32 devices in a mesh: turn: 8 (over z, y), col: 4 (over x, core).
Axes of the slice: x: 2, y: 2, z: 4, core: 2. Of those that a mesh axis runs over, the one named last changes fastest.
Arguments:
- right_sides: float32 [16, 256, 512], P('turn', 'col'), may hold values from -6 to 6
- fill_blocks: bfloat16 [16, 2, 256, 256], P('turn', None, None, 'col'), may hold values from -0.1875 to 0.1875
Outputs:
- reduced: float32 [16, 256, 512], P('turn', 'col')
The draws below stay inside these ranges and needn't reach their ends.
All inputs are finite; a program needn't handle non-finite values.
Results may differ from the reference program's by a relative error of at most 0.0022.
Values may be sent and summed in bfloat16 or wider, within the bound.
A program may use at most 64 MiB of HBM per device.

```python
import jax
import jax.numpy as jnp
from jax import lax

B = 256
R = 512
LEVELS = 4
TURNS = 16


def block_levels(stream_key, shape, split, smallest, high):
    loudness, own = 1.0, jax.random.fold_in(stream_key, 6)
    for position, parts in split:
        heights = jnp.exp(jax.random.uniform(jax.random.fold_in(own, position), (parts,), jnp.float32, smallest / len(split), high / len(split)))
        loudness = loudness * jnp.repeat(heights, shape[position] // parts).reshape([-1 if axis == position else 1 for axis in range(len(shape))])
    return loudness


def bell_draw(rng, extent, width, most, cuts=(), kind=jnp.bfloat16):
    gain = block_levels(rng, extent, cuts, -0.22, 0.18) if cuts else 1.0
    drawn = jax.random.normal(rng, extent, jnp.float32) * width * gain
    return jnp.minimum(jnp.maximum(drawn, -most), most).astype(kind)


def setup_inputs(seed: int = 0) -> dict:
    keys = jax.random.split(jax.random.key(seed), 3)
    right_sides = bell_draw(keys[0], (TURNS, B, R), 1.0, 6.0, ((0, 8), (1, 4)), jnp.float32)
    fill_blocks = bell_draw(keys[1], (TURNS, 2, B, B), (4 * B) ** -0.5, 0.1875, ((0, 8), (3, 4)))
    return dict(right_sides=right_sides, fill_blocks=fill_blocks)


def reference(right_sides, fill_blocks):
    state = right_sides
    for level_num in range(LEVELS):
        half_step = 2 ** level_num
        stride = 2 * half_step
        rounded = lax.optimization_barrier(state[half_step::stride].astype(jnp.bfloat16))
        source_rows = rounded.astype(jnp.float32)
        source_fill = fill_blocks[half_step::stride].astype(jnp.float32)
        to_left = jnp.einsum("mab,mbr->mar", source_fill[:, 0], source_rows, precision=lax.Precision.HIGHEST)
        to_right = jnp.einsum("mab,mbr->mar", source_fill[:, 1], source_rows, precision=lax.Precision.HIGHEST)
        from_right = jnp.concatenate([jnp.zeros_like(to_right[:1]), to_right[:-1]], axis=0)
        kept_rows = state[::stride] - (to_left + from_right)
        state = state.at[::stride].set(kept_rows)
    return state
```

```python
import functools

import jax
import jax.numpy as jnp
from jax import lax
from jax.experimental import pallas as pl
from jax.experimental.pallas import tpu as pltpu
from jax.sharding import PartitionSpec as P

LEVELS = 4
MESH = pl.DeviceIdType.MESH
F32 = jnp.float32
BF16 = jnp.bfloat16


def kernel(T, C, rs_ref, fill_ref, out_ref, pk, qs, q0, st, acc, cs0, cs, r0, rv, fin, ao,
           ph_s, ph_r, l0_s, l0_r, ch_s, ch_r, fi_s, fi_r, ao_s, ao_r):
    b, r = q0.shape[1], q0.shape[2]
    half = fill_ref.shape[3]
    p, c = lax.axis_index("turn"), lax.axis_index("col")
    last = LEVELS - 1

    def is_source(k):
        d = 2 ** (k - 1)
        return lax.rem(p, 2 * d) == d

    def is_kept(k):
        return lax.rem(p, 2 ** k) == 0

    def in_level(k):
        return lax.rem(p, 2 ** (k - 1)) == 0

    barrier = pltpu.get_barrier_semaphore()

    def greet(pt, pc):
        pl.semaphore_signal(barrier, inc=1, device_id=(pt, pc), device_id_type=MESH)

    peers = [lax.rem(c + off, C) for off in range(1, C)]
    for pc in peers:
        greet(p, pc)
    count = jnp.int32(C - 1)
    for k in range(1, LEVELS):
        d = 2 ** (k - 1)
        for there, pt in ((p >= d, p - d), (p + d < T, p + d)):
            cond = jnp.logical_and(in_level(k), there)

            @pl.when(cond)
            def _():
                greet(pt, c)
                if k == last:
                    for pc in peers:
                        greet(pt, pc)

            count = count + jnp.where(cond, C if k == last else 1, 0)

    par = lax.rem(c, 2)
    for l in (1, 0):
        pk[1 - l, c] = jnp.concatenate([fill_ref[l, par], fill_ref[l, 1 - par]], axis=-1)
        if l == 1:
            for i in range(C):
                qs[i] = rs_ref[1, :, i * r:(i + 1) * r].astype(BF16)
            q0[c] = qs[c]

    own = pl.ds(pl.multiple_of(c * r, r), r)
    st[c] = rs_ref[0, :, own]
    pl.semaphore_wait(barrier, count)

    def rcopy(src, dst, ss, rr, pt, pc):
        return pltpu.make_async_remote_copy(
            src_ref=src, dst_ref=dst, send_sem=ss, recv_sem=rr, device_id=(pt, pc), device_id_type=MESH)

    def phase(kind, off):
        pc = peers[off - 1]
        if kind == 0:
            src, dst = pk.at[0, c], pk.at[0, c]
        elif kind == 1:
            src, dst = qs.at[pc], q0.at[c]
        elif kind == 2:
            src, dst = rs_ref.at[0, :, pl.ds(pl.multiple_of(pc * r, r), r)], st.at[c]
        else:
            src, dst = pk.at[1, c], pk.at[1, c]
        return rcopy(src, dst, ph_s.at[kind, off - 1], ph_r.at[kind, off - 1], p, pc)

    offs = list(range(1, C))
    for kind in (0, 1, 2, 3):
        for off in offs:
            phase(kind, off).start()


    def fills(l):
        w = [pk[l, i] for i in range(C)]
        low = lax.broadcasted_iota(jnp.int32, w[0].shape, 1) < half
        left = jnp.concatenate([jnp.where(low, w[i], w[i + 1]) for i in range(0, C, 2)], axis=-1)
        right = jnp.concatenate([jnp.where(low, w[i + 1], w[i]) for i in range(0, C, 2)], axis=-1)
        return left, right

    def swap(q):
        return jnp.concatenate([q[(i ^ 1) * b:((i ^ 1) + 1) * b] for i in range(C)], axis=0)

    def dot(f, q):
        return jnp.dot(f, q, preferred_element_type=F32)

    for kind in (0, 1):
        for off in offs:
            phase(kind, off).wait_recv()
    left0, right0 = fills(0)
    q = jnp.concatenate([q0[i] for i in range(C)], axis=0)
    cs0[...] = dot(right0, swap(q))
    has_right, has_left = p + 1 < T, p >= 1
    send0 = rcopy(cs0, r0, l0_s, l0_r, p + 1, c)

    @pl.when(has_right)
    def _():
        send0.start()

    acc[...] = dot(left0, q)
    for kind in (2, 3):
        for off in offs:
            phase(kind, off).wait_recv()

    @pl.when(has_left)
    def _():
        rcopy(cs0, r0, l0_s, l0_r, p, c).wait_recv()
        acc[...] += r0[...]

    def piece(i):
        return pl.ds(pl.multiple_of(i * b, b), b)

    def out_copy(off):
        pc = peers[off - 1]
        return rcopy(acc.at[piece(pc)], ao.at[c], ao_s.at[off - 1], ao_r.at[off - 1], p, pc)

    def start_out():
        for off in offs:
            out_copy(off).start()
        ao[c] = acc[piece(c)]

    def chain_copy(k, side):
        d = 2 ** (k - 1)
        return rcopy(cs.at[side], rv.at[k - 1, side], ch_s.at[side], ch_r.at[k - 1, side],
                     p - d if side == 0 else p + d, c)

    def final_copy(side, i):
        d = 2 ** (last - 1)
        return rcopy(cs.at[side, piece(i)], fin.at[side, c], fi_s.at[side, i], fi_r.at[side, c],
                     p - d if side == 0 else p + d, i)

    def final_recv(side, i):
        return rcopy(cs.at[side, piece(0)], fin.at[side, i], fi_s.at[side, i], fi_r.at[side, i], p, i)

    for k in range(1, LEVELS):
        d = 2 ** (k - 1)

        @pl.when(is_source(k))
        def _():
            state = jnp.concatenate([st[i] for i in range(C)], axis=0) - acc[...]
            qk = state.astype(BF16)
            left1, right1 = fills(1)
            cs[0] = dot(left1, qk)
            if k == last:
                for i in range(C):
                    final_copy(0, i).start()
            else:
                chain_copy(k, 0).start()

            @pl.when(p + d < T)
            def _():
                cs[1] = dot(right1, swap(qk))
                if k == last:
                    for i in range(C):
                        final_copy(1, i).start()
                else:
                    chain_copy(k, 1).start()

            start_out()

        @pl.when(is_kept(k))
        def _():
            if k == last:
                start_out()
            else:
                @pl.when(p + d < T)
                def _():
                    chain_copy(k, 0).wait_recv()
                    acc[...] += rv[k - 1, 0]

                @pl.when(p >= d)
                def _():
                    chain_copy(k, 1).wait_recv()
                    acc[...] += rv[k - 1, 1]

    out_ref[1] = rs_ref[1]
    for off in offs:
        out_copy(off).wait_recv()
    for i in range(C):
        cols = slice(i * r, (i + 1) * r)
        out_ref[0, :, cols] = rs_ref[0, :, cols] - ao[i]
    D = 2 ** (last - 1)
    for side, there in ((0, p + D < T), (1, p >= D)):
        @pl.when(jnp.logical_and(is_kept(last), there))
        def _():
            for i in range(C):
                final_recv(side, i).wait_recv()
                cols = slice(i * r, (i + 1) * r)
                out_ref[0, :, cols] -= fin[side, i]

    for kind in range(4):
        for off in offs:
            phase(kind, off).wait_send()

    @pl.when(has_right)
    def _():
        send0.wait_send()

    for k in range(1, LEVELS):
        d = 2 ** (k - 1)
        for side, there in ((0, p >= d), (1, p + d < T)):
            @pl.when(jnp.logical_and(is_source(k), there))
            def _():
                if k == last:
                    for i in range(C):
                        final_copy(side, i).wait_send()
                else:
                    chain_copy(k, side).wait_send()
    for off in offs:
        out_copy(off).wait_send()


def shards(T, C, right_sides, fill_blocks):
    _, b, R = right_sides.shape
    B = fill_blocks.shape[2]
    r = R // C
    dma = pltpu.SemaphoreType.DMA
    vm = pl.BlockSpec(memory_space=pltpu.VMEM)
    return pl.pallas_call(
        functools.partial(kernel, T, C),
        out_shape=jax.ShapeDtypeStruct(right_sides.shape, F32),
        in_specs=[vm, vm],
        out_specs=vm,
        scratch_shapes=[
            pltpu.VMEM((2, C, B, 2 * fill_blocks.shape[3]), BF16),
            pltpu.VMEM((C, b, r), BF16),
            pltpu.VMEM((C, b, r), BF16),
            pltpu.VMEM((C, b, r), F32),
            pltpu.VMEM((B, r), F32),
            pltpu.VMEM((B, r), F32),
            pltpu.VMEM((2, B, r), F32),
            pltpu.VMEM((B, r), F32),
            pltpu.VMEM((LEVELS - 1, 2, B, r), F32),
            pltpu.VMEM((2, C, b, r), F32),
            pltpu.VMEM((C, b, r), F32),
            dma((4, C - 1)), dma((4, C - 1)),
            dma, dma,
            dma((2,)), dma((LEVELS - 1, 2)),
            dma((2, C)), dma((2, C)),
            dma((C - 1,)), dma((C - 1,)),
        ],
        compiler_params=pltpu.CompilerParams(collective_id=0, has_side_effects=True),
    )(right_sides, fill_blocks)


def solution(mesh):
    placed = (P("turn", "col", None), P("turn", None, None, "col"))
    return jax.shard_map(
        functools.partial(shards, mesh.shape["turn"], mesh.shape["col"]),
        mesh=mesh, in_specs=placed, out_specs=P("turn", "col", None), check_vma=False
    )
```

```python
import functools

import jax
import jax.numpy as jnp
from jax import lax
from jax.experimental import pallas as pl
from jax.experimental.pallas import tpu as pltpu
from jax.sharding import PartitionSpec as P

LEVELS = 4
MESH = pl.DeviceIdType.MESH
F32 = jnp.float32
BF16 = jnp.bfloat16


def kernel(T, C, rs_ref, fill_ref, out_ref, g0, qs, q0, st, acc, g, tf, tl, qb, qv, cs, fin, ao,
           ab_s, ab_r, cd_s, cd_r, st_s, st_r, fp_s, fp_r, fw_s, fw_r, ch_s, ch_r, fi_s, fi_r, ao_s, ao_r):
    b, r = st.shape[1], st.shape[2]
    p, c = lax.axis_index("turn"), lax.axis_index("col")
    last = LEVELS - 1
    offs = list(range(1, C))
    peers = [None] + [lax.rem(c + off, C) for off in offs]

    def is_source(k):
        d = 2 ** (k - 1)
        return lax.rem(p, 2 * d) == d

    def is_kept(k):
        return lax.rem(p, 2 ** k) == 0

    def in_level(k):
        return lax.rem(p, 2 ** (k - 1)) == 0

    def to(k, side):
        d = 2 ** (k - 1)
        return p - d if side == 0 else p + d

    def target(k, side):
        d = 2 ** (k - 1)
        return p >= d if side == 0 else p + d < T

    def sends(k, side):
        return jnp.logical_and(is_source(k), target(k, side))

    def receives(k, side):
        return jnp.logical_and(is_kept(k), target(k, 1 - side))

    barrier = pltpu.get_barrier_semaphore()

    def greet(pt, pc):
        pl.semaphore_signal(barrier, inc=1, device_id=(pt, pc), device_id_type=MESH)

    for off in offs:
        greet(p, peers[off])
    count = jnp.int32(C - 1)
    for k in range(1, LEVELS):
        wide = k == 1 or k == last
        for side in range(2):
            cond = jnp.logical_and(in_level(k), target(k, side))

            @pl.when(cond)
            def _():
                greet(to(k, side), c)
                if wide:
                    for off in offs:
                        greet(to(k, side), peers[off])

            count = count + jnp.where(cond, C if wide else 1, 0)

    for i in range(C):
        qs[i] = rs_ref[1, :, i * r:(i + 1) * r].astype(BF16)
    q0[0, c] = qs[c]
    g0[0, c] = fill_ref[1, 0]

    def columns(i):
        return pl.ds(pl.multiple_of(i * r, r), r)

    def piece(i):
        return pl.ds(pl.multiple_of(i * b, b), b)

    st[c] = rs_ref[0, :, columns(c)]
    for side in range(2):
        @pl.when(sends(last, side))
        def _():
            g[last - 1, side, c] = fill_ref[0, side]

    pl.semaphore_wait(barrier, count)

    def rcopy(src, dst, ss, rr, pt, pc):
        return pltpu.make_async_remote_copy(
            src_ref=src, dst_ref=dst, send_sem=ss, recv_sem=rr, device_id=(pt, pc), device_id_type=MESH)

    def own_fill(off):
        return rcopy(fill_ref.at[1, 0], g0.at[0, c], ab_s.at[0, off - 1], ab_r.at[0, off - 1], p, peers[off])

    def own_q(off):
        return rcopy(qs.at[peers[off]], q0.at[0, c], ab_s.at[1, off - 1], ab_r.at[1, off - 1], p, peers[off])

    def next_fill(off):
        pc = c if off == 0 else peers[off]
        return rcopy(fill_ref.at[1, 1], g0.at[1, c], cd_s.at[0, off], cd_r.at[0, off], p + 1, pc)

    def next_q(off):
        pc = c if off == 0 else peers[off]
        return rcopy(qs.at[pc], q0.at[1, c], cd_s.at[1, off], cd_r.at[1, off], p + 1, pc)

    def state_copy(off):
        return rcopy(rs_ref.at[0, :, columns(peers[off])], st.at[c], st_s.at[off - 1], st_r.at[off - 1], p, peers[off])

    def fill_piece(k, side):
        return rcopy(fill_ref.at[0, side], g.at[k - 1, side, c], fp_s.at[side], fp_r.at[k - 1, side], to(k, side), c)

    def forward(k, side, off):
        return rcopy(g.at[k - 1, side, c], g.at[k - 1, side, c],
                     fw_s.at[k - 1, side, off - 1], fw_r.at[k - 1, side, off - 1], p, peers[off])

    later = lax.rem(p, 2 ** last) > 0
    has_right, has_left = p + 1 < T, p >= 1

    @pl.when(has_right)
    def _():
        for off in offs + [0]:
            next_fill(off).start()
            next_q(off).start()

    for off in offs:
        own_fill(off).start()
        own_q(off).start()
    for k in range(1, last):
        for side in (1, 0):
            @pl.when(sends(k, side))
            def _():
                fill_piece(k, side).start()

    @pl.when(later)
    def _():
        for off in offs:
            state_copy(off).start()

    for k in range(1, last):
        for side in range(2):
            @pl.when(receives(k, side))
            def _():
                fill_piece(k, side).wait_recv()
                for off in offs:
                    forward(k, side, off).start()

    for side in range(2):
        @pl.when(sends(last, side))
        def _():
            for off in offs:
                forward(last, side, off).start()

    def whole(ref):
        return jnp.concatenate([ref[i] for i in range(C)], axis=0)

    def dot(f, q):
        return jnp.dot(f, q, preferred_element_type=F32)

    for off in offs:
        own_fill(off).wait_recv()
        own_q(off).wait_recv()
    acc[...] = dot(whole(g0.at[0]).T, whole(q0.at[0]))

    @pl.when(has_left)
    def _():
        for off in [0] + offs:
            next_fill(off).wait_recv()
            next_q(off).wait_recv()
        acc[...] += dot(whole(g0.at[1]).T, whole(q0.at[1]))

    def out_copy(off):
        return rcopy(acc.at[piece(peers[off])], ao.at[c], ao_s.at[off - 1], ao_r.at[off - 1], p, peers[off])

    def start_out():
        for off in offs:
            out_copy(off).start()
        ao[c] = acc[piece(c)]

    def chain_copy(k, side):
        return rcopy(qb, qv.at[k - 1, side], ch_s.at[side], ch_r.at[k - 1, side], to(k, side), c)

    def final_copy(side, i):
        return rcopy(cs.at[side, piece(i)], fin.at[side, c], fi_s.at[side, i], fi_r.at[side, c], to(last, side), i)

    def final_recv(side, i):
        return rcopy(cs.at[side, piece(0)], fin.at[side, i], fi_s.at[side, i], fi_r.at[side, i], p, i)

    @pl.when(later)
    def _():
        for off in offs:
            state_copy(off).wait_recv()

    for k in range(1, LEVELS):
        if k == last - 1:
            for side in range(2):
                @pl.when(sends(last, side))
                def _():
                    for off in offs:
                        forward(last, side, off).wait_recv()
                    tl[side] = whole(g.at[last - 1, side]).T

        if k < last:
            for side in range(2):
                @pl.when(receives(k, side))
                def _():
                    for off in offs:
                        forward(k, side, off).wait_recv()
                    tf[side] = whole(g.at[k - 1, side]).T

        @pl.when(is_source(k))
        def _():
            qk = (whole(st) - acc[...]).astype(BF16)
            if k < last:
                qb[...] = qk
            for side in (1, 0):
                @pl.when(target(k, side))
                def _():
                    if k == last:
                        cs[side] = dot(tl[side], qk)
                        for i in range(C):
                            final_copy(side, i).start()
                    else:
                        chain_copy(k, side).start()

            start_out()

        if k < last:
            for side in range(2):
                @pl.when(receives(k, side))
                def _():
                    chain_copy(k, side).wait_recv()
                    acc[...] += dot(tf[side], qv[k - 1, side])
        else:
            @pl.when(is_kept(k))
            def _():
                start_out()

    for off in offs:
        out_copy(off).wait_recv()
    for i in range(C):
        out_ref[:, i * r:(i + 1) * r] = ao[i]
    for side in range(2):
        @pl.when(receives(last, side))
        def _():
            for i in range(C):
                final_recv(side, i).wait_recv()
                out_ref[:, i * r:(i + 1) * r] += fin[side, i]

    for off in offs:
        own_fill(off).wait_send()
        own_q(off).wait_send()
        out_copy(off).wait_send()

    @pl.when(has_right)
    def _():
        for off in [0] + offs:
            next_fill(off).wait_send()
            next_q(off).wait_send()

    @pl.when(later)
    def _():
        for off in offs:
            state_copy(off).wait_send()

    for k in range(1, LEVELS):
        for side in range(2):
            @pl.when(sends(k, side))
            def _():
                if k == last:
                    for i in range(C):
                        final_copy(side, i).wait_send()
                    for off in offs:
                        forward(k, side, off).wait_send()
                else:
                    fill_piece(k, side).wait_send()
                    chain_copy(k, side).wait_send()

            if k < last:
                @pl.when(receives(k, side))
                def _():
                    for off in offs:
                        forward(k, side, off).wait_send()


def shards(T, C, right_sides, fill_blocks):
    _, b, R = right_sides.shape
    B = fill_blocks.shape[2]
    r = R // C
    n = fill_blocks.shape[3]
    dma = pltpu.SemaphoreType.DMA
    vm = pl.BlockSpec(memory_space=pltpu.VMEM)
    update = pl.pallas_call(
        functools.partial(kernel, T, C),
        out_shape=jax.ShapeDtypeStruct((b, R), F32),
        in_specs=[vm, vm],
        out_specs=vm,
        scratch_shapes=[
            pltpu.VMEM((2, C, n, B), BF16),
            pltpu.VMEM((C, b, r), BF16),
            pltpu.VMEM((2, C, b, r), BF16),
            pltpu.VMEM((C, b, r), F32),
            pltpu.VMEM((B, r), F32),
            pltpu.VMEM((LEVELS - 1, 2, C, n, B), BF16),
            pltpu.VMEM((2, B, B), BF16),
            pltpu.VMEM((2, B, B), BF16),
            pltpu.VMEM((B, r), BF16),
            pltpu.VMEM((LEVELS - 2, 2, B, r), BF16),
            pltpu.VMEM((2, B, r), F32),
            pltpu.VMEM((2, C, b, r), F32),
            pltpu.VMEM((C, b, r), F32),
            dma((2, C - 1)), dma((2, C - 1)),
            dma((2, C)), dma((2, C)),
            dma((C - 1,)), dma((C - 1,)),
            dma((2,)), dma((LEVELS - 2, 2)),
            dma((LEVELS - 1, 2, C - 1)), dma((LEVELS - 1, 2, C - 1)),
            dma((2,)), dma((LEVELS - 2, 2)),
            dma((2, C)), dma((2, C)),
            dma((C - 1,)), dma((C - 1,)),
        ],
        compiler_params=pltpu.CompilerParams(collective_id=0, has_side_effects=True),
    )(right_sides, jnp.swapaxes(fill_blocks, 2, 3))
    return right_sides - jnp.pad(update[None], ((0, 1), (0, 0), (0, 0)))


def solution(mesh):
    placed = (P("turn", "col", None), P("turn", None, None, "col"))
    return jax.shard_map(
        functools.partial(shards, mesh.shape["turn"], mesh.shape["col"]),
        mesh=mesh, in_specs=placed, out_specs=P("turn", "col", None), check_vma=False
    )
```

```python
import functools

import jax
import jax.numpy as jnp
from jax import lax
from jax.experimental import pallas as pl
from jax.experimental.pallas import tpu as pltpu
from jax.sharding import PartitionSpec as P

LEVELS = 4
MESH = pl.DeviceIdType.MESH
F32 = jnp.float32
BF16 = jnp.bfloat16


def kernel(T, C, rs_ref, fill_ref, out_ref, g0, qs, q0, st, acc, g, tf, tl, qb, qv, cs, fin, ao,
           ab_s, ab_r, cd_s, cd_r, st_s, st_r, fp_s, fp_r, fw_s, fw_r, ch_s, ch_r, fi_s, fi_r, ao_s, ao_r):
    b, r = st.shape[1], st.shape[2]
    p, c = lax.axis_index("turn"), lax.axis_index("col")
    last = LEVELS - 1
    offs = list(range(1, C))
    peers = [None] + [lax.rem(c + off, C) for off in offs]
    H = C // 2
    partner = c + 1 - 2 * lax.rem(c, 2)
    rest = [0] + list(range(H, C - 1))

    def is_source(k):
        d = 2 ** (k - 1)
        return lax.rem(p, 2 * d) == d

    def is_kept(k):
        return lax.rem(p, 2 ** k) == 0

    def in_level(k):
        return lax.rem(p, 2 ** (k - 1)) == 0

    def to(k, side):
        d = 2 ** (k - 1)
        return p - d if side == 0 else p + d

    def target(k, side):
        d = 2 ** (k - 1)
        return p >= d if side == 0 else p + d < T

    def sends(k, side):
        return jnp.logical_and(is_source(k), target(k, side))

    def receives(k, side):
        return jnp.logical_and(is_kept(k), target(k, 1 - side))

    barrier = pltpu.get_barrier_semaphore()

    def greet(pt, pc):
        pl.semaphore_signal(barrier, inc=1, device_id=(pt, pc), device_id_type=MESH)

    for off in offs:
        greet(p, peers[off])
    count = jnp.int32(C - 1)
    for k in range(1, LEVELS):
        wide = k == 1 or k == last
        for side in range(2):
            cond = jnp.logical_and(in_level(k), target(k, side))

            @pl.when(cond)
            def _():
                greet(to(k, side), c)
                if wide:
                    for off in offs:
                        greet(to(k, side), peers[off])

            count = count + jnp.where(cond, C if wide else 1, 0)

    for i in range(C):
        qs[i] = rs_ref[1, :, i * r:(i + 1) * r].astype(BF16)
    q0[0, c] = qs[c]
    g0[0, c] = fill_ref[1, 0]

    def columns(i):
        return pl.ds(pl.multiple_of(i * r, r), r)

    def piece(i):
        return pl.ds(pl.multiple_of(i * b, b), b)

    st[c] = rs_ref[0, :, columns(c)]
    for side in range(2):
        @pl.when(sends(last, side))
        def _():
            g[last - 1, side, c] = fill_ref[0, side]

    pl.semaphore_wait(barrier, count)

    def rcopy(src, dst, ss, rr, pt, pc):
        return pltpu.make_async_remote_copy(
            src_ref=src, dst_ref=dst, send_sem=ss, recv_sem=rr, device_id=(pt, pc), device_id_type=MESH)

    def passed(j):
        return lax.rem(c - 2 * j + C, C)

    def own_fill(i):
        ss, rr = ab_s.at[0, i], ab_r.at[0, i]
        if i < H:
            return rcopy(fill_ref.at[1, 0], g0.at[0, c], ss, rr, p, peers[2 * i] if i else partner)
        slot = g0.at[0, passed(i - H + 1)]
        return rcopy(slot, slot, ss, rr, p, partner)

    def own_q(off):
        return rcopy(qs.at[peers[off]], q0.at[0, c], ab_s.at[1, off - 1], ab_r.at[1, off - 1], p, peers[off])

    def next_fill(i):
        ss, rr = cd_s.at[0, i], cd_r.at[0, i]
        if i < H:
            return rcopy(fill_ref.at[1, 1], g0.at[1, c], ss, rr, p + 1, peers[2 * i] if i else c)
        slot = g0.at[1, passed(i - H)]
        return rcopy(slot, slot, ss, rr, p, partner)

    def next_q(off):
        pc = c if off == 0 else peers[off]
        return rcopy(qs.at[pc], q0.at[1, c], cd_s.at[1, off], cd_r.at[1, off], p + 1, pc)

    def state_copy(off):
        return rcopy(rs_ref.at[0, :, columns(peers[off])], st.at[c], st_s.at[off - 1], st_r.at[off - 1], p, peers[off])

    def fill_piece(k, side):
        return rcopy(fill_ref.at[0, side], g.at[k - 1, side, c], fp_s.at[side], fp_r.at[k - 1, side], to(k, side), c)

    def forward(k, side, i):
        slot = g.at[k - 1, side, c if i < H else passed(i - H + 1)]
        pc = partner if i == 0 or i >= H else peers[2 * i]
        return rcopy(slot, slot, fw_s.at[k - 1, side, i], fw_r.at[k - 1, side, i], p, pc)

    def relay(copy):
        for i in range(1, H):
            copy(i).wait_recv()
            copy(H + i - 1).start()

    later = lax.rem(p, 2 ** last) > 0
    has_right, has_left = p + 1 < T, p >= 1

    @pl.when(has_right)
    def _():
        for i in reversed(range(H)):
            next_fill(i).start()

    for i in reversed(range(H)):
        own_fill(i).start()

    @pl.when(has_right)
    def _():
        for off in offs + [0]:
            next_q(off).start()

    for off in offs:
        own_q(off).start()
    for k in range(1, last):
        for side in (1, 0):
            @pl.when(sends(k, side))
            def _():
                fill_piece(k, side).start()

    @pl.when(later)
    def _():
        for off in offs:
            state_copy(off).start()

    for k in range(1, last):
        for side in range(2):
            @pl.when(receives(k, side))
            def _():
                fill_piece(k, side).wait_recv()
                for i in reversed(range(H)):
                    forward(k, side, i).start()

    for side in range(2):
        @pl.when(sends(last, side))
        def _():
            for i in reversed(range(H)):
                forward(last, side, i).start()

    def whole(ref):
        return jnp.concatenate([ref[i] for i in range(C)], axis=0)

    def dot(f, q):
        return jnp.dot(f, q, preferred_element_type=F32)

    relay(own_fill)

    @pl.when(has_left)
    def _():
        for i in range(H):
            next_fill(i).wait_recv()
            next_fill(H + i).start()

    for i in rest:
        own_fill(i).wait_recv()
    for off in offs:
        own_q(off).wait_recv()
    acc[...] = dot(whole(g0.at[0]).T, whole(q0.at[0]))

    @pl.when(has_left)
    def _():
        for i in range(H, C):
            next_fill(i).wait_recv()
        for off in [0] + offs:
            next_q(off).wait_recv()
        acc[...] += dot(whole(g0.at[1]).T, whole(q0.at[1]))

    for k in range(1, LEVELS):
        for side in range(2):
            @pl.when(receives(k, side) if k < last else sends(k, side))
            def _():
                relay(functools.partial(forward, k, side))

    def out_copy(off):
        return rcopy(acc.at[piece(peers[off])], ao.at[c], ao_s.at[off - 1], ao_r.at[off - 1], p, peers[off])

    def start_out():
        for off in offs:
            out_copy(off).start()
        ao[c] = acc[piece(c)]

    def chain_copy(k, side):
        return rcopy(qb, qv.at[k - 1, side], ch_s.at[side], ch_r.at[k - 1, side], to(k, side), c)

    def final_copy(side, i):
        return rcopy(cs.at[side, piece(i)], fin.at[side, c], fi_s.at[side, i], fi_r.at[side, c], to(last, side), i)

    def final_recv(side, i):
        return rcopy(cs.at[side, piece(0)], fin.at[side, i], fi_s.at[side, i], fi_r.at[side, i], p, i)

    @pl.when(later)
    def _():
        for off in offs:
            state_copy(off).wait_recv()

    for k in range(1, LEVELS):
        if k == last - 1:
            for side in range(2):
                @pl.when(sends(last, side))
                def _():
                    for i in rest:
                        forward(last, side, i).wait_recv()
                    tl[side] = whole(g.at[last - 1, side]).T

        if k < last:
            for side in range(2):
                @pl.when(receives(k, side))
                def _():
                    for i in rest:
                        forward(k, side, i).wait_recv()
                    tf[side] = whole(g.at[k - 1, side]).T

        @pl.when(is_source(k))
        def _():
            qk = (whole(st) - acc[...]).astype(BF16)
            if k < last:
                qb[...] = qk
            for side in (1, 0):
                @pl.when(target(k, side))
                def _():
                    if k == last:
                        cs[side] = dot(tl[side], qk)
                        for i in range(C):
                            final_copy(side, i).start()
                    else:
                        chain_copy(k, side).start()

            start_out()

        if k < last:
            for side in range(2):
                @pl.when(receives(k, side))
                def _():
                    chain_copy(k, side).wait_recv()
                    acc[...] += dot(tf[side], qv[k - 1, side])
        else:
            @pl.when(is_kept(k))
            def _():
                start_out()

    for off in offs:
        out_copy(off).wait_recv()
    for i in range(C):
        out_ref[:, i * r:(i + 1) * r] = ao[i]
    for side in range(2):
        @pl.when(receives(last, side))
        def _():
            for i in range(C):
                final_recv(side, i).wait_recv()
                out_ref[:, i * r:(i + 1) * r] += fin[side, i]

    for i in range(C - 1):
        own_fill(i).wait_send()
    for off in offs:
        own_q(off).wait_send()
        out_copy(off).wait_send()

    @pl.when(has_right)
    def _():
        for i in range(H):
            next_fill(i).wait_send()
        for off in [0] + offs:
            next_q(off).wait_send()

    @pl.when(has_left)
    def _():
        for i in range(H, C):
            next_fill(i).wait_send()

    @pl.when(later)
    def _():
        for off in offs:
            state_copy(off).wait_send()

    for k in range(1, LEVELS):
        for side in range(2):
            @pl.when(sends(k, side))
            def _():
                if k == last:
                    for i in range(C):
                        final_copy(side, i).wait_send()
                    for i in range(C - 1):
                        forward(k, side, i).wait_send()
                else:
                    fill_piece(k, side).wait_send()
                    chain_copy(k, side).wait_send()

            if k < last:
                @pl.when(receives(k, side))
                def _():
                    for i in range(C - 1):
                        forward(k, side, i).wait_send()


def shards(T, C, right_sides, fill_blocks):
    _, b, R = right_sides.shape
    B = fill_blocks.shape[2]
    r = R // C
    n = fill_blocks.shape[3]
    dma = pltpu.SemaphoreType.DMA
    vm = pl.BlockSpec(memory_space=pltpu.VMEM)
    update = pl.pallas_call(
        functools.partial(kernel, T, C),
        out_shape=jax.ShapeDtypeStruct((b, R), F32),
        in_specs=[vm, vm],
        out_specs=vm,
        scratch_shapes=[
            pltpu.VMEM((2, C, n, B), BF16),
            pltpu.VMEM((C, b, r), BF16),
            pltpu.VMEM((2, C, b, r), BF16),
            pltpu.VMEM((C, b, r), F32),
            pltpu.VMEM((B, r), F32),
            pltpu.VMEM((LEVELS - 1, 2, C, n, B), BF16),
            pltpu.VMEM((2, B, B), BF16),
            pltpu.VMEM((2, B, B), BF16),
            pltpu.VMEM((B, r), BF16),
            pltpu.VMEM((LEVELS - 2, 2, B, r), BF16),
            pltpu.VMEM((2, B, r), F32),
            pltpu.VMEM((2, C, b, r), F32),
            pltpu.VMEM((C, b, r), F32),
            dma((2, C - 1)), dma((2, C - 1)),
            dma((2, C)), dma((2, C)),
            dma((C - 1,)), dma((C - 1,)),
            dma((2,)), dma((LEVELS - 2, 2)),
            dma((LEVELS - 1, 2, C - 1)), dma((LEVELS - 1, 2, C - 1)),
            dma((2,)), dma((LEVELS - 2, 2)),
            dma((2, C)), dma((2, C)),
            dma((C - 1,)), dma((C - 1,)),
        ],
        compiler_params=pltpu.CompilerParams(collective_id=0, has_side_effects=True),
    )(right_sides, jnp.swapaxes(fill_blocks, 2, 3))
    return right_sides - jnp.pad(update[None], ((0, 1), (0, 0), (0, 0)))


def solution(mesh):
    placed = (P("turn", "col", None), P("turn", None, None, "col"))
    return jax.shard_map(
        functools.partial(shards, mesh.shape["turn"], mesh.shape["col"]),
        mesh=mesh, in_specs=placed, out_specs=P("turn", "col", None), check_vma=False
    )
```

```python
import functools

import jax
import jax.numpy as jnp
from jax import lax
from jax.experimental import pallas as pl
from jax.experimental.pallas import tpu as pltpu
from jax.sharding import PartitionSpec as P

LEVELS = 4
MESH = pl.DeviceIdType.MESH
F32 = jnp.float32
BF16 = jnp.bfloat16


def kernel(T, C, rs_ref, fill_ref, out_ref, g0, qs, q0, st, acc, g, tf, tl, qb, qv, cs, fin, ao,
           ab_s, ab_r, cd_s, cd_r, st_s, st_r, fp_s, fp_r, fw_s, fw_r, ch_s, ch_r, fi_s, fi_r, ao_s, ao_r):
    b, r = st.shape[1], st.shape[2]
    p, c = lax.axis_index("turn"), lax.axis_index("col")
    last = LEVELS - 1
    offs = list(range(1, C))
    peers = [None] + [lax.rem(c + off, C) for off in offs]
    H = C // 2
    partner = c + 1 - 2 * lax.rem(c, 2)
    rest = [0] + list(range(H, C - 1))

    def is_source(k):
        d = 2 ** (k - 1)
        return lax.rem(p, 2 * d) == d

    def is_kept(k):
        return lax.rem(p, 2 ** k) == 0

    def in_level(k):
        return lax.rem(p, 2 ** (k - 1)) == 0

    def to(k, side):
        d = 2 ** (k - 1)
        return p - d if side == 0 else p + d

    def target(k, side):
        d = 2 ** (k - 1)
        return p >= d if side == 0 else p + d < T

    def sends(k, side):
        return jnp.logical_and(is_source(k), target(k, side))

    def receives(k, side):
        return jnp.logical_and(is_kept(k), target(k, 1 - side))

    barrier = pltpu.get_barrier_semaphore()

    def greet(pt, pc):
        pl.semaphore_signal(barrier, inc=1, device_id=(pt, pc), device_id_type=MESH)

    for off in offs:
        greet(p, peers[off])
    count = jnp.int32(C - 1)
    for k in range(1, LEVELS):
        wide = k == 1 or k == last
        for side in range(2):
            cond = jnp.logical_and(in_level(k), target(k, side))

            @pl.when(cond)
            def _():
                greet(to(k, side), c)
                if wide:
                    for off in offs:
                        greet(to(k, side), peers[off])

            count = count + jnp.where(cond, C if wide else 1, 0)

    for i in range(C):
        qs[i] = rs_ref[1, :, i * r:(i + 1) * r].astype(BF16)
    q0[0, c] = qs[c]
    g0[0, c] = fill_ref[1, 0]

    def columns(i):
        return pl.ds(pl.multiple_of(i * r, r), r)

    def piece(i):
        return pl.ds(pl.multiple_of(i * b, b), b)

    st[c] = rs_ref[0, :, columns(c)]
    for side in range(2):
        @pl.when(sends(last, side))
        def _():
            g[last - 1, side, c] = fill_ref[0, side]

    pl.semaphore_wait(barrier, count)

    def rcopy(src, dst, ss, rr, pt, pc):
        return pltpu.make_async_remote_copy(
            src_ref=src, dst_ref=dst, send_sem=ss, recv_sem=rr, device_id=(pt, pc), device_id_type=MESH)

    def passed(j):
        return lax.rem(c - 2 * j + C, C)

    def own_fill(i):
        ss, rr = ab_s.at[0, i], ab_r.at[0, i]
        if i < H:
            return rcopy(fill_ref.at[1, 0], g0.at[0, c], ss, rr, p, peers[2 * i] if i else partner)
        slot = g0.at[0, passed(i - H + 1)]
        return rcopy(slot, slot, ss, rr, p, partner)

    def own_q(off):
        return rcopy(qs.at[peers[off]], q0.at[0, c], ab_s.at[1, off - 1], ab_r.at[1, off - 1], p, peers[off])

    def next_fill(i):
        ss, rr = cd_s.at[0, i], cd_r.at[0, i]
        if i < H:
            return rcopy(fill_ref.at[1, 1], g0.at[1, c], ss, rr, p + 1, peers[2 * i] if i else c)
        slot = g0.at[1, passed(i - H)]
        return rcopy(slot, slot, ss, rr, p, partner)

    def next_q(off):
        pc = c if off == 0 else peers[off]
        return rcopy(qs.at[pc], q0.at[1, c], cd_s.at[1, off], cd_r.at[1, off], p + 1, pc)

    def state_copy(off):
        return rcopy(rs_ref.at[0, :, columns(peers[off])], st.at[c], st_s.at[off - 1], st_r.at[off - 1], p, peers[off])

    def fill_piece(k, side):
        return rcopy(fill_ref.at[0, side], g.at[k - 1, side, c], fp_s.at[side], fp_r.at[k - 1, side], to(k, side), c)

    def forward(k, side, i):
        slot = g.at[k - 1, side, c if i < H else passed(i - H + 1)]
        pc = partner if i == 0 or i >= H else peers[2 * i]
        return rcopy(slot, slot, fw_s.at[k - 1, side, i], fw_r.at[k - 1, side, i], p, pc)

    def relay(copy):
        for i in range(1, H):
            copy(i).wait_recv()
            copy(H + i - 1).start()

    later = lax.rem(p, 2 ** last) > 0
    has_right, has_left = p + 1 < T, p >= 1

    @pl.when(has_right)
    def _():
        for i in reversed(range(H)):
            next_fill(i).start()

    for i in reversed(range(H)):
        own_fill(i).start()

    @pl.when(has_right)
    def _():
        for off in offs + [0]:
            next_q(off).start()

    for off in offs:
        own_q(off).start()
    for k in range(1, last):
        for side in (1, 0):
            @pl.when(sends(k, side))
            def _():
                fill_piece(k, side).start()

    @pl.when(later)
    def _():
        for off in offs:
            state_copy(off).start()

    for k in range(1, last):
        for side in range(2):
            @pl.when(receives(k, side))
            def _():
                fill_piece(k, side).wait_recv()
                for i in reversed(range(H)):
                    forward(k, side, i).start()

    for side in range(2):
        @pl.when(sends(last, side))
        def _():
            for i in reversed(range(H)):
                forward(last, side, i).start()

    def whole(ref):
        return jnp.concatenate([ref[i] for i in range(C)], axis=0)

    def dot(f, q):
        return jnp.dot(f, q, preferred_element_type=F32)

    relay(own_fill)

    @pl.when(has_left)
    def _():
        for i in range(H):
            next_fill(i).wait_recv()
            next_fill(H + i).start()

    for i in rest:
        own_fill(i).wait_recv()
    for off in offs:
        own_q(off).wait_recv()
    acc[...] = dot(whole(g0.at[0]).T, whole(q0.at[0]))

    @pl.when(has_left)
    def _():
        for i in range(H, C):
            next_fill(i).wait_recv()
        for off in [0] + offs:
            next_q(off).wait_recv()
        acc[...] += dot(whole(g0.at[1]).T, whole(q0.at[1]))

    for k in range(1, LEVELS):
        for side in range(2):
            @pl.when(receives(k, side) if k < last else sends(k, side))
            def _():
                relay(functools.partial(forward, k, side))

    def out_copy(off):
        return rcopy(acc.at[piece(peers[off])], ao.at[c], ao_s.at[off - 1], ao_r.at[off - 1], p, peers[off])

    def start_out():
        for off in offs:
            out_copy(off).start()
        ao[c] = acc[piece(c)]

    def chain_copy(k, side):
        return rcopy(qb, qv.at[k - 1, side], ch_s.at[side], ch_r.at[k - 1, side], to(k, side), c)

    def final_copy(side, i):
        return rcopy(cs.at[side, piece(i)], fin.at[side, c], fi_s.at[side, i], fi_r.at[side, c], to(last, side), i)

    def final_recv(side, i):
        return rcopy(cs.at[side, piece(0)], fin.at[side, i], fi_s.at[side, i], fi_r.at[side, i], p, i)

    @pl.when(later)
    def _():
        for off in offs:
            state_copy(off).wait_recv()

    for k in range(1, LEVELS):
        if k == last - 1:
            for side in range(2):
                @pl.when(sends(last, side))
                def _():
                    for i in rest:
                        forward(last, side, i).wait_recv()
                    tl[side] = whole(g.at[last - 1, side]).T

        if k < last:
            for side in range(2):
                @pl.when(receives(k, side))
                def _():
                    for i in rest:
                        forward(k, side, i).wait_recv()
                    tf[side] = whole(g.at[k - 1, side]).T

        @pl.when(is_source(k))
        def _():
            qk = (whole(st) - acc[...]).astype(BF16)
            if k < last:
                qb[...] = qk
            for side in (1, 0):
                @pl.when(target(k, side))
                def _():
                    if k == last:
                        cs[side] = dot(tl[side], qk).astype(BF16)
                        for i in range(C):
                            final_copy(side, i).start()
                    else:
                        chain_copy(k, side).start()

            start_out()

        if k < last:
            for side in range(2):
                @pl.when(receives(k, side))
                def _():
                    chain_copy(k, side).wait_recv()
                    acc[...] += dot(tf[side], qv[k - 1, side])
        else:
            @pl.when(is_kept(k))
            def _():
                start_out()

    for off in offs:
        out_copy(off).wait_recv()
    for i in range(C):
        out_ref[:, i * r:(i + 1) * r] = ao[i]
    for side in range(2):
        @pl.when(receives(last, side))
        def _():
            for i in range(C):
                final_recv(side, i).wait_recv()
                out_ref[:, i * r:(i + 1) * r] += fin[side, i].astype(F32)

    for i in range(C - 1):
        own_fill(i).wait_send()
    for off in offs:
        own_q(off).wait_send()
        out_copy(off).wait_send()

    @pl.when(has_right)
    def _():
        for i in range(H):
            next_fill(i).wait_send()
        for off in [0] + offs:
            next_q(off).wait_send()

    @pl.when(has_left)
    def _():
        for i in range(H, C):
            next_fill(i).wait_send()

    @pl.when(later)
    def _():
        for off in offs:
            state_copy(off).wait_send()

    for k in range(1, LEVELS):
        for side in range(2):
            @pl.when(sends(k, side))
            def _():
                if k == last:
                    for i in range(C):
                        final_copy(side, i).wait_send()
                    for i in range(C - 1):
                        forward(k, side, i).wait_send()
                else:
                    fill_piece(k, side).wait_send()
                    chain_copy(k, side).wait_send()

            if k < last:
                @pl.when(receives(k, side))
                def _():
                    for i in range(C - 1):
                        forward(k, side, i).wait_send()


def shards(T, C, right_sides, fill_blocks):
    _, b, R = right_sides.shape
    B = fill_blocks.shape[2]
    r = R // C
    n = fill_blocks.shape[3]
    dma = pltpu.SemaphoreType.DMA
    vm = pl.BlockSpec(memory_space=pltpu.VMEM)
    update = pl.pallas_call(
        functools.partial(kernel, T, C),
        out_shape=jax.ShapeDtypeStruct((b, R), F32),
        in_specs=[vm, vm],
        out_specs=vm,
        scratch_shapes=[
            pltpu.VMEM((2, C, n, B), BF16),
            pltpu.VMEM((C, b, r), BF16),
            pltpu.VMEM((2, C, b, r), BF16),
            pltpu.VMEM((C, b, r), F32),
            pltpu.VMEM((B, r), F32),
            pltpu.VMEM((LEVELS - 1, 2, C, n, B), BF16),
            pltpu.VMEM((2, B, B), BF16),
            pltpu.VMEM((2, B, B), BF16),
            pltpu.VMEM((B, r), BF16),
            pltpu.VMEM((LEVELS - 2, 2, B, r), BF16),
            pltpu.VMEM((2, B, r), BF16),
            pltpu.VMEM((2, C, b, r), BF16),
            pltpu.VMEM((C, b, r), F32),
            dma((2, C - 1)), dma((2, C - 1)),
            dma((2, C)), dma((2, C)),
            dma((C - 1,)), dma((C - 1,)),
            dma((2,)), dma((LEVELS - 2, 2)),
            dma((LEVELS - 1, 2, C - 1)), dma((LEVELS - 1, 2, C - 1)),
            dma((2,)), dma((LEVELS - 2, 2)),
            dma((2, C)), dma((2, C)),
            dma((C - 1,)), dma((C - 1,)),
        ],
        compiler_params=pltpu.CompilerParams(collective_id=0, has_side_effects=True),
    )(right_sides, jnp.swapaxes(fill_blocks, 2, 3))
    return right_sides - jnp.pad(update[None], ((0, 1), (0, 0), (0, 0)))


def solution(mesh):
    placed = (P("turn", "col", None), P("turn", None, None, "col"))
    return jax.shard_map(
        functools.partial(shards, mesh.shape["turn"], mesh.shape["col"]),
        mesh=mesh, in_specs=placed, out_specs=P("turn", "col", None), check_vma=False
    )
```

```python
import functools

import jax
import jax.numpy as jnp
from jax import lax
from jax.experimental import pallas as pl
from jax.experimental.pallas import tpu as pltpu
from jax.sharding import PartitionSpec as P

LEVELS = 4
MESH = pl.DeviceIdType.MESH
F32 = jnp.float32
BF16 = jnp.bfloat16


def kernel(T, C, rs_hbm, fill_hbm, out_ref, rs_ref, fill_ref, in_s, g0, qs, q0, st, acc, g, tf, tl, qb, qv, cs, fin, ao,
           ab_s, ab_r, cd_s, cd_r, st_s, st_r, fp_s, fp_r, fw_s, fw_r, ch_s, ch_r, fi_s, fi_r, ao_s, ao_r):
    b, r = st.shape[1], st.shape[2]
    p, c = lax.axis_index("turn"), lax.axis_index("col")
    last = LEVELS - 1
    offs = list(range(1, C))
    peers = [None] + [lax.rem(c + off, C) for off in offs]
    H = C // 2
    partner = c + 1 - 2 * lax.rem(c, 2)
    rest = [0] + list(range(H, C - 1))

    def is_source(k):
        d = 2 ** (k - 1)
        return lax.rem(p, 2 * d) == d

    def is_kept(k):
        return lax.rem(p, 2 ** k) == 0

    def in_level(k):
        return lax.rem(p, 2 ** (k - 1)) == 0

    def to(k, side):
        d = 2 ** (k - 1)
        return p - d if side == 0 else p + d

    def target(k, side):
        d = 2 ** (k - 1)
        return p >= d if side == 0 else p + d < T

    def sends(k, side):
        return jnp.logical_and(is_source(k), target(k, side))

    def receives(k, side):
        return jnp.logical_and(is_kept(k), target(k, 1 - side))

    loads = [pltpu.make_async_copy(rs_hbm.at[1], rs_ref.at[1], in_s.at[0]),
             pltpu.make_async_copy(fill_hbm, fill_ref, in_s.at[1]),
             pltpu.make_async_copy(rs_hbm.at[0], rs_ref.at[0], in_s.at[2])]
    for load in loads:
        load.start()

    barrier = pltpu.get_barrier_semaphore()

    def greet(pt, pc):
        pl.semaphore_signal(barrier, inc=1, device_id=(pt, pc), device_id_type=MESH)

    for off in offs:
        greet(p, peers[off])
    count = jnp.int32(C - 1)
    for k in range(1, LEVELS):
        wide = k == 1 or k == last
        for side in range(2):
            cond = jnp.logical_and(in_level(k), target(k, side))

            @pl.when(cond)
            def _():
                greet(to(k, side), c)
                if wide:
                    for off in offs:
                        greet(to(k, side), peers[off])

            count = count + jnp.where(cond, C if wide else 1, 0)

    for load in loads:
        load.wait()
    for i in range(C):
        qs[i] = rs_ref[1, :, i * r:(i + 1) * r].astype(BF16)
    q0[0, c] = qs[c]
    g0[0, c] = fill_ref[1, 0]

    def columns(i):
        return pl.ds(pl.multiple_of(i * r, r), r)

    def piece(i):
        return pl.ds(pl.multiple_of(i * b, b), b)

    st[c] = rs_ref[0, :, columns(c)]
    for side in range(2):
        @pl.when(sends(last, side))
        def _():
            g[last - 1, side, c] = fill_ref[0, side]

    pl.semaphore_wait(barrier, count)

    def rcopy(src, dst, ss, rr, pt, pc):
        return pltpu.make_async_remote_copy(
            src_ref=src, dst_ref=dst, send_sem=ss, recv_sem=rr, device_id=(pt, pc), device_id_type=MESH)

    def passed(j):
        return lax.rem(c - 2 * j + C, C)

    def own_fill(i):
        ss, rr = ab_s.at[0, i], ab_r.at[0, i]
        if i < H:
            return rcopy(fill_ref.at[1, 0], g0.at[0, c], ss, rr, p, peers[2 * i] if i else partner)
        slot = g0.at[0, passed(i - H + 1)]
        return rcopy(slot, slot, ss, rr, p, partner)

    def own_q(off):
        return rcopy(qs.at[peers[off]], q0.at[0, c], ab_s.at[1, off - 1], ab_r.at[1, off - 1], p, peers[off])

    def next_fill(i):
        ss, rr = cd_s.at[0, i], cd_r.at[0, i]
        if i < H:
            return rcopy(fill_ref.at[1, 1], g0.at[1, c], ss, rr, p + 1, peers[2 * i] if i else c)
        slot = g0.at[1, passed(i - H)]
        return rcopy(slot, slot, ss, rr, p, partner)

    def next_q(off):
        pc = c if off == 0 else peers[off]
        return rcopy(qs.at[pc], q0.at[1, c], cd_s.at[1, off], cd_r.at[1, off], p + 1, pc)

    def state_copy(off):
        return rcopy(rs_ref.at[0, :, columns(peers[off])], st.at[c], st_s.at[off - 1], st_r.at[off - 1], p, peers[off])

    def fill_piece(k, side):
        return rcopy(fill_ref.at[0, side], g.at[k - 1, side, c], fp_s.at[side], fp_r.at[k - 1, side], to(k, side), c)

    def forward(k, side, i):
        slot = g.at[k - 1, side, c if i < H else passed(i - H + 1)]
        pc = partner if i == 0 or i >= H else peers[2 * i]
        return rcopy(slot, slot, fw_s.at[k - 1, side, i], fw_r.at[k - 1, side, i], p, pc)

    def relay(copy):
        for i in range(1, H):
            copy(i).wait_recv()
            copy(H + i - 1).start()

    later = lax.rem(p, 2 ** last) > 0
    has_right, has_left = p + 1 < T, p >= 1

    @pl.when(has_right)
    def _():
        for i in reversed(range(H)):
            next_fill(i).start()

    for i in reversed(range(H)):
        own_fill(i).start()

    @pl.when(has_right)
    def _():
        for off in offs + [0]:
            next_q(off).start()

    for off in offs:
        own_q(off).start()
    for k in range(1, last):
        for side in (1, 0):
            @pl.when(sends(k, side))
            def _():
                fill_piece(k, side).start()

    @pl.when(later)
    def _():
        for off in offs:
            state_copy(off).start()

    for k in range(1, last):
        for side in range(2):
            @pl.when(receives(k, side))
            def _():
                fill_piece(k, side).wait_recv()
                for i in reversed(range(H)):
                    forward(k, side, i).start()

    for side in range(2):
        @pl.when(sends(last, side))
        def _():
            for i in reversed(range(H)):
                forward(last, side, i).start()

    def whole(ref):
        return jnp.concatenate([ref[i] for i in range(C)], axis=0)

    def dot(f, q):
        return jnp.dot(f, q, preferred_element_type=F32)

    relay(own_fill)

    @pl.when(has_left)
    def _():
        for i in range(H):
            next_fill(i).wait_recv()
            next_fill(H + i).start()

    for i in rest:
        own_fill(i).wait_recv()
    for off in offs:
        own_q(off).wait_recv()
    acc[...] = dot(whole(g0.at[0]).T, whole(q0.at[0]))

    @pl.when(has_left)
    def _():
        for i in range(H, C):
            next_fill(i).wait_recv()
        for off in [0] + offs:
            next_q(off).wait_recv()
        acc[...] += dot(whole(g0.at[1]).T, whole(q0.at[1]))

    for k in range(1, LEVELS):
        for side in range(2):
            @pl.when(receives(k, side) if k < last else sends(k, side))
            def _():
                relay(functools.partial(forward, k, side))

    def out_copy(off):
        return rcopy(acc.at[piece(peers[off])], ao.at[c], ao_s.at[off - 1], ao_r.at[off - 1], p, peers[off])

    def start_out():
        for off in offs:
            out_copy(off).start()
        ao[c] = acc[piece(c)]

    def chain_copy(k, side):
        return rcopy(qb, qv.at[k - 1, side], ch_s.at[side], ch_r.at[k - 1, side], to(k, side), c)

    def final_copy(side, i):
        return rcopy(cs.at[side, piece(i)], fin.at[side, c], fi_s.at[side, i], fi_r.at[side, c], to(last, side), i)

    def final_recv(side, i):
        return rcopy(cs.at[side, piece(0)], fin.at[side, i], fi_s.at[side, i], fi_r.at[side, i], p, i)

    @pl.when(later)
    def _():
        for off in offs:
            state_copy(off).wait_recv()

    for k in range(1, LEVELS):
        if k == last - 1:
            for side in range(2):
                @pl.when(sends(last, side))
                def _():
                    for i in rest:
                        forward(last, side, i).wait_recv()
                    tl[side] = whole(g.at[last - 1, side]).T

        if k < last:
            for side in range(2):
                @pl.when(receives(k, side))
                def _():
                    for i in rest:
                        forward(k, side, i).wait_recv()
                    tf[side] = whole(g.at[k - 1, side]).T

        @pl.when(is_source(k))
        def _():
            qk = (whole(st) - acc[...]).astype(BF16)
            if k < last:
                qb[...] = qk
            for side in (1, 0):
                @pl.when(target(k, side))
                def _():
                    if k == last:
                        cs[side] = dot(tl[side], qk)
                        for i in range(C):
                            final_copy(side, i).start()
                    else:
                        chain_copy(k, side).start()

            start_out()

        if k < last:
            for side in range(2):
                @pl.when(receives(k, side))
                def _():
                    chain_copy(k, side).wait_recv()
                    acc[...] += dot(tf[side], qv[k - 1, side])
        else:
            @pl.when(is_kept(k))
            def _():
                start_out()

    for off in offs:
        out_copy(off).wait_recv()
    for i in range(C):
        out_ref[:, i * r:(i + 1) * r] = ao[i]
    for side in range(2):
        @pl.when(receives(last, side))
        def _():
            for i in range(C):
                final_recv(side, i).wait_recv()
                out_ref[:, i * r:(i + 1) * r] += fin[side, i]

    for i in range(C - 1):
        own_fill(i).wait_send()
    for off in offs:
        own_q(off).wait_send()
        out_copy(off).wait_send()

    @pl.when(has_right)
    def _():
        for i in range(H):
            next_fill(i).wait_send()
        for off in [0] + offs:
            next_q(off).wait_send()

    @pl.when(has_left)
    def _():
        for i in range(H, C):
            next_fill(i).wait_send()

    @pl.when(later)
    def _():
        for off in offs:
            state_copy(off).wait_send()

    for k in range(1, LEVELS):
        for side in range(2):
            @pl.when(sends(k, side))
            def _():
                if k == last:
                    for i in range(C):
                        final_copy(side, i).wait_send()
                    for i in range(C - 1):
                        forward(k, side, i).wait_send()
                else:
                    fill_piece(k, side).wait_send()
                    chain_copy(k, side).wait_send()

            if k < last:
                @pl.when(receives(k, side))
                def _():
                    for i in range(C - 1):
                        forward(k, side, i).wait_send()


def shards(T, C, right_sides, fill_blocks):
    _, b, R = right_sides.shape
    B = fill_blocks.shape[2]
    r = R // C
    n = fill_blocks.shape[3]
    dma = pltpu.SemaphoreType.DMA
    vm = pl.BlockSpec(memory_space=pltpu.VMEM)
    update = pl.pallas_call(
        functools.partial(kernel, T, C),
        out_shape=jax.ShapeDtypeStruct((b, R), F32),
        in_specs=[pl.BlockSpec(memory_space=pl.ANY)] * 2,
        out_specs=vm,
        scratch_shapes=[
            pltpu.VMEM(right_sides.shape, F32),
            pltpu.VMEM((2, 2, n, B), BF16),
            dma((3,)),
            pltpu.VMEM((2, C, n, B), BF16),
            pltpu.VMEM((C, b, r), BF16),
            pltpu.VMEM((2, C, b, r), BF16),
            pltpu.VMEM((C, b, r), F32),
            pltpu.VMEM((B, r), F32),
            pltpu.VMEM((LEVELS - 1, 2, C, n, B), BF16),
            pltpu.VMEM((2, B, B), BF16),
            pltpu.VMEM((2, B, B), BF16),
            pltpu.VMEM((B, r), BF16),
            pltpu.VMEM((LEVELS - 2, 2, B, r), BF16),
            pltpu.VMEM((2, B, r), F32),
            pltpu.VMEM((2, C, b, r), F32),
            pltpu.VMEM((C, b, r), F32),
            dma((2, C - 1)), dma((2, C - 1)),
            dma((2, C)), dma((2, C)),
            dma((C - 1,)), dma((C - 1,)),
            dma((2,)), dma((LEVELS - 2, 2)),
            dma((LEVELS - 1, 2, C - 1)), dma((LEVELS - 1, 2, C - 1)),
            dma((2,)), dma((LEVELS - 2, 2)),
            dma((2, C)), dma((2, C)),
            dma((C - 1,)), dma((C - 1,)),
        ],
        compiler_params=pltpu.CompilerParams(collective_id=0, has_side_effects=True),
    )(right_sides, jnp.swapaxes(fill_blocks, 2, 3))
    return right_sides - jnp.pad(update[None], ((0, 1), (0, 0), (0, 0)))


def solution(mesh):
    placed = (P("turn", "col", None), P("turn", None, None, "col"))
    return jax.shard_map(
        functools.partial(shards, mesh.shape["turn"], mesh.shape["col"]),
        mesh=mesh, in_specs=placed, out_specs=P("turn", "col", None), check_vma=False
    )
```

```python
import functools

import jax
import jax.numpy as jnp
from jax import lax
from jax.experimental import pallas as pl
from jax.experimental.pallas import tpu as pltpu
from jax.sharding import PartitionSpec as P

LEVELS = 4
MESH = pl.DeviceIdType.MESH
F32 = jnp.float32
BF16 = jnp.bfloat16


def kernel(T, C, rs_hbm, fill_hbm, out_ref, rs_ref, fill_ref, in_s, g0, qs, q0, st, acc, g, tf, tl, qb, qv, cs, fin, ao,
           ab_s, ab_r, cd_s, cd_r, st_s, st_r, fp_s, fp_r, fw_s, fw_r, ch_s, ch_r, fi_s, fi_r, ao_s, ao_r):
    b, r = st.shape[1], st.shape[2]
    p, c = lax.axis_index("turn"), lax.axis_index("col")
    last = LEVELS - 1
    offs = list(range(1, C))
    peers = [None] + [lax.rem(c + off, C) for off in offs]
    H = C // 2
    partner = c + 1 - 2 * lax.rem(c, 2)
    rest = [0] + list(range(H, C - 1))

    def is_source(k):
        d = 2 ** (k - 1)
        return lax.rem(p, 2 * d) == d

    def is_kept(k):
        return lax.rem(p, 2 ** k) == 0

    def in_level(k):
        return lax.rem(p, 2 ** (k - 1)) == 0

    def to(k, side):
        d = 2 ** (k - 1)
        return p - d if side == 0 else p + d

    def target(k, side):
        d = 2 ** (k - 1)
        return p >= d if side == 0 else p + d < T

    def sends(k, side):
        return jnp.logical_and(is_source(k), target(k, side))

    def receives(k, side):
        return jnp.logical_and(is_kept(k), target(k, 1 - side))

    loads = [pltpu.make_async_copy(rs_hbm.at[1], rs_ref.at[1], in_s.at[0]),
             pltpu.make_async_copy(fill_hbm, fill_ref, in_s.at[1]),
             pltpu.make_async_copy(rs_hbm.at[0], rs_ref.at[0], in_s.at[2])]
    for load in loads:
        load.start()

    barrier = pltpu.get_barrier_semaphore()

    def greet(pt, pc):
        pl.semaphore_signal(barrier, inc=1, device_id=(pt, pc), device_id_type=MESH)

    for off in offs:
        greet(p, peers[off])
    count = jnp.int32(C - 1)
    for k in range(1, LEVELS):
        wide = k == 1 or k == last
        for side in range(2):
            cond = jnp.logical_and(in_level(k), target(k, side))

            @pl.when(cond)
            def _():
                greet(to(k, side), c)
                if wide:
                    for off in offs:
                        greet(to(k, side), peers[off])

            count = count + jnp.where(cond, C if wide else 1, 0)

    for load in loads:
        load.wait()
    for i in range(C):
        qs[i] = rs_ref[1, :, i * r:(i + 1) * r].astype(BF16)
    q0[0, c] = qs[c]
    g0[0, c] = fill_ref[1, 0]

    def columns(i):
        return pl.ds(pl.multiple_of(i * r, r), r)

    def piece(i):
        return pl.ds(pl.multiple_of(i * b, b), b)

    st[c] = rs_ref[0, :, columns(c)]
    for side in range(2):
        @pl.when(sends(last, side))
        def _():
            g[last - 1, side, c] = fill_ref[0, side]

    pl.semaphore_wait(barrier, count)

    def rcopy(src, dst, ss, rr, pt, pc):
        return pltpu.make_async_remote_copy(
            src_ref=src, dst_ref=dst, send_sem=ss, recv_sem=rr, device_id=(pt, pc), device_id_type=MESH)

    def passed(j):
        return lax.rem(c - 2 * j + C, C)

    def own_fill(i):
        ss, rr = ab_s.at[0, i], ab_r.at[0, i]
        if i < H:
            return rcopy(fill_ref.at[1, 0], g0.at[0, c], ss, rr, p, peers[2 * i] if i else partner)
        slot = g0.at[0, passed(i - H + 1)]
        return rcopy(slot, slot, ss, rr, p, partner)

    def own_q(off):
        return rcopy(qs.at[peers[off]], q0.at[0, c], ab_s.at[1, off - 1], ab_r.at[1, off - 1], p, peers[off])

    def next_fill(i):
        ss, rr = cd_s.at[0, i], cd_r.at[0, i]
        if i < H:
            return rcopy(fill_ref.at[1, 1], g0.at[1, c], ss, rr, p + 1, peers[2 * i] if i else c)
        slot = g0.at[1, passed(i - H)]
        return rcopy(slot, slot, ss, rr, p, partner)

    def next_q(off):
        pc = c if off == 0 else peers[off]
        return rcopy(qs.at[pc], q0.at[1, c], cd_s.at[1, off], cd_r.at[1, off], p + 1, pc)

    def state_copy(off):
        return rcopy(rs_ref.at[0, :, columns(peers[off])], st.at[c], st_s.at[off - 1], st_r.at[off - 1], p, peers[off])

    def fill_piece(k, side):
        return rcopy(fill_ref.at[0, side], g.at[k - 1, side, c], fp_s.at[side], fp_r.at[k - 1, side], to(k, side), c)

    def forward(k, side, i):
        slot = g.at[k - 1, side, c if i < H else passed(i - H + 1)]
        pc = partner if i == 0 or i >= H else peers[2 * i]
        return rcopy(slot, slot, fw_s.at[k - 1, side, i], fw_r.at[k - 1, side, i], p, pc)

    def relay(copy):
        for i in range(1, H):
            copy(i).wait_recv()
            copy(H + i - 1).start()

    later = lax.rem(p, 2 ** last) > 0
    has_right, has_left = p + 1 < T, p >= 1

    def start_next_fill():
        @pl.when(has_right)
        def _():
            for i in reversed(range(H)):
                next_fill(i).start()

    def start_next_q():
        @pl.when(has_right)
        def _():
            for off in offs + [0]:
                next_q(off).start()

    def start_own_fill():
        for i in reversed(range(H)):
            own_fill(i).start()

    def start_own_q():
        for off in offs:
            own_q(off).start()

    def start_state():
        @pl.when(later)
        def _():
            for off in offs:
                state_copy(off).start()

    def start_pieces(k):
        for side in (1, 0):
            @pl.when(sends(k, side))
            def _():
                fill_piece(k, side).start()

    @pl.when(is_source(1))
    def _():
        start_own_fill()
        start_own_q()
        start_state()
        start_pieces(1)
        start_next_fill()
        start_next_q()

    @pl.when(is_kept(1))
    def _():
        start_next_fill()
        start_own_fill()
        start_next_q()
        start_own_q()
        for k in range(2, last):
            start_pieces(k)
        start_state()

    for k in range(1, last):
        for side in range(2):
            @pl.when(receives(k, side))
            def _():
                fill_piece(k, side).wait_recv()
                for i in reversed(range(H)):
                    forward(k, side, i).start()

    for side in range(2):
        @pl.when(sends(last, side))
        def _():
            for i in reversed(range(H)):
                forward(last, side, i).start()

    def whole(ref):
        return jnp.concatenate([ref[i] for i in range(C)], axis=0)

    def dot(f, q):
        return jnp.dot(f, q, preferred_element_type=F32)

    relay(own_fill)

    @pl.when(has_left)
    def _():
        for i in range(H):
            next_fill(i).wait_recv()
            next_fill(H + i).start()

    for i in rest:
        own_fill(i).wait_recv()
    for off in offs:
        own_q(off).wait_recv()
    acc[...] = dot(whole(g0.at[0]).T, whole(q0.at[0]))

    @pl.when(has_left)
    def _():
        for i in range(H, C):
            next_fill(i).wait_recv()
        for off in [0] + offs:
            next_q(off).wait_recv()
        acc[...] += dot(whole(g0.at[1]).T, whole(q0.at[1]))

    for k in range(1, LEVELS):
        for side in range(2):
            @pl.when(receives(k, side) if k < last else sends(k, side))
            def _():
                relay(functools.partial(forward, k, side))

    def out_copy(off):
        return rcopy(acc.at[piece(peers[off])], ao.at[c], ao_s.at[off - 1], ao_r.at[off - 1], p, peers[off])

    def start_out():
        for off in offs:
            out_copy(off).start()
        ao[c] = acc[piece(c)]

    def chain_copy(k, side):
        return rcopy(qb, qv.at[k - 1, side], ch_s.at[side], ch_r.at[k - 1, side], to(k, side), c)

    def final_copy(side, i):
        return rcopy(cs.at[side, piece(i)], fin.at[side, c], fi_s.at[side, i], fi_r.at[side, c], to(last, side), i)

    def final_recv(side, i):
        return rcopy(cs.at[side, piece(0)], fin.at[side, i], fi_s.at[side, i], fi_r.at[side, i], p, i)

    @pl.when(later)
    def _():
        for off in offs:
            state_copy(off).wait_recv()

    for k in range(1, LEVELS):
        if k == last - 1:
            for side in range(2):
                @pl.when(sends(last, side))
                def _():
                    for i in rest:
                        forward(last, side, i).wait_recv()
                    tl[side] = whole(g.at[last - 1, side]).T

        if k < last:
            for side in range(2):
                @pl.when(receives(k, side))
                def _():
                    for i in rest:
                        forward(k, side, i).wait_recv()
                    tf[side] = whole(g.at[k - 1, side]).T

        @pl.when(is_source(k))
        def _():
            qk = (whole(st) - acc[...]).astype(BF16)
            if k < last:
                qb[...] = qk
            for side in (1, 0):
                @pl.when(target(k, side))
                def _():
                    if k == last:
                        cs[side] = dot(tl[side], qk)
                        for i in range(C):
                            final_copy(side, i).start()
                    else:
                        chain_copy(k, side).start()

            start_out()

        if k < last:
            for side in range(2):
                @pl.when(receives(k, side))
                def _():
                    chain_copy(k, side).wait_recv()
                    acc[...] += dot(tf[side], qv[k - 1, side])
        else:
            @pl.when(is_kept(k))
            def _():
                start_out()

    for off in offs:
        out_copy(off).wait_recv()
    for i in range(C):
        out_ref[:, i * r:(i + 1) * r] = ao[i]
    for side in range(2):
        @pl.when(receives(last, side))
        def _():
            for i in range(C):
                final_recv(side, i).wait_recv()
                out_ref[:, i * r:(i + 1) * r] += fin[side, i]

    for i in range(C - 1):
        own_fill(i).wait_send()
    for off in offs:
        own_q(off).wait_send()
        out_copy(off).wait_send()

    @pl.when(has_right)
    def _():
        for i in range(H):
            next_fill(i).wait_send()
        for off in [0] + offs:
            next_q(off).wait_send()

    @pl.when(has_left)
    def _():
        for i in range(H, C):
            next_fill(i).wait_send()

    @pl.when(later)
    def _():
        for off in offs:
            state_copy(off).wait_send()

    for k in range(1, LEVELS):
        for side in range(2):
            @pl.when(sends(k, side))
            def _():
                if k == last:
                    for i in range(C):
                        final_copy(side, i).wait_send()
                    for i in range(C - 1):
                        forward(k, side, i).wait_send()
                else:
                    fill_piece(k, side).wait_send()
                    chain_copy(k, side).wait_send()

            if k < last:
                @pl.when(receives(k, side))
                def _():
                    for i in range(C - 1):
                        forward(k, side, i).wait_send()


def shards(T, C, right_sides, fill_blocks):
    _, b, R = right_sides.shape
    B = fill_blocks.shape[2]
    r = R // C
    n = fill_blocks.shape[3]
    dma = pltpu.SemaphoreType.DMA
    vm = pl.BlockSpec(memory_space=pltpu.VMEM)
    update = pl.pallas_call(
        functools.partial(kernel, T, C),
        out_shape=jax.ShapeDtypeStruct((b, R), F32),
        in_specs=[pl.BlockSpec(memory_space=pl.ANY)] * 2,
        out_specs=vm,
        scratch_shapes=[
            pltpu.VMEM(right_sides.shape, F32),
            pltpu.VMEM((2, 2, n, B), BF16),
            dma((3,)),
            pltpu.VMEM((2, C, n, B), BF16),
            pltpu.VMEM((C, b, r), BF16),
            pltpu.VMEM((2, C, b, r), BF16),
            pltpu.VMEM((C, b, r), F32),
            pltpu.VMEM((B, r), F32),
            pltpu.VMEM((LEVELS - 1, 2, C, n, B), BF16),
            pltpu.VMEM((2, B, B), BF16),
            pltpu.VMEM((2, B, B), BF16),
            pltpu.VMEM((B, r), BF16),
            pltpu.VMEM((LEVELS - 2, 2, B, r), BF16),
            pltpu.VMEM((2, B, r), F32),
            pltpu.VMEM((2, C, b, r), F32),
            pltpu.VMEM((C, b, r), F32),
            dma((2, C - 1)), dma((2, C - 1)),
            dma((2, C)), dma((2, C)),
            dma((C - 1,)), dma((C - 1,)),
            dma((2,)), dma((LEVELS - 2, 2)),
            dma((LEVELS - 1, 2, C - 1)), dma((LEVELS - 1, 2, C - 1)),
            dma((2,)), dma((LEVELS - 2, 2)),
            dma((2, C)), dma((2, C)),
            dma((C - 1,)), dma((C - 1,)),
        ],
        compiler_params=pltpu.CompilerParams(collective_id=0, has_side_effects=True),
    )(right_sides, jnp.swapaxes(fill_blocks, 2, 3))
    return right_sides - jnp.pad(update[None], ((0, 1), (0, 0), (0, 0)))


def solution(mesh):
    placed = (P("turn", "col", None), P("turn", None, None, "col"))
    return jax.shard_map(
        functools.partial(shards, mesh.shape["turn"], mesh.shape["col"]),
        mesh=mesh, in_specs=placed, out_specs=P("turn", "col", None), check_vma=False
    )
```

```python
import functools

import jax
import jax.numpy as jnp
from jax import lax
from jax.experimental import pallas as pl
from jax.experimental.pallas import tpu as pltpu
from jax.sharding import PartitionSpec as P

LEVELS = 4
MESH = pl.DeviceIdType.MESH
F32 = jnp.float32
BF16 = jnp.bfloat16


def kernel(T, C, rs_hbm, fill_hbm, out_ref, rs_ref, fill_ref, in_s, g0, qs, q0, st, acc, g, tf, tl, qb, qv, cs, fin, ao,
           ab_s, ab_r, cd_s, cd_r, st_s, st_r, fp_s, fp_r, fw_s, fw_r, ch_s, ch_r, fi_s, fi_r, ao_s, ao_r):
    b, r = st.shape[1], st.shape[2]
    p, c = lax.axis_index("turn"), lax.axis_index("col")
    last = LEVELS - 1
    offs = list(range(1, C))
    peers = [None] + [lax.rem(c + off, C) for off in offs]
    H = C // 2
    partner = c + 1 - 2 * lax.rem(c, 2)
    rest = [0] + list(range(H, C - 1))

    def is_source(k):
        d = 2 ** (k - 1)
        return lax.rem(p, 2 * d) == d

    def is_kept(k):
        return lax.rem(p, 2 ** k) == 0

    def in_level(k):
        return lax.rem(p, 2 ** (k - 1)) == 0

    def to(k, side):
        d = 2 ** (k - 1)
        return p - d if side == 0 else p + d

    def target(k, side):
        d = 2 ** (k - 1)
        return p >= d if side == 0 else p + d < T

    def sends(k, side):
        return jnp.logical_and(is_source(k), target(k, side))

    def receives(k, side):
        return jnp.logical_and(is_kept(k), target(k, 1 - side))

    loads = [pltpu.make_async_copy(rs_hbm.at[1], rs_ref.at[1], in_s.at[0]),
             pltpu.make_async_copy(fill_hbm, fill_ref, in_s.at[1]),
             pltpu.make_async_copy(rs_hbm.at[0], rs_ref.at[0], in_s.at[2])]
    for load in loads:
        load.start()

    barrier = pltpu.get_barrier_semaphore()

    def greet(pt, pc):
        pl.semaphore_signal(barrier, inc=1, device_id=(pt, pc), device_id_type=MESH)

    for off in offs:
        greet(p, peers[off])
    count = jnp.int32(C - 1)
    for k in range(1, LEVELS):
        wide = k == 1 or k == last
        for side in range(2):
            cond = jnp.logical_and(in_level(k), target(k, side))

            @pl.when(cond)
            def _():
                greet(to(k, side), c)
                if wide:
                    for off in offs:
                        greet(to(k, side), peers[off])

            count = count + jnp.where(cond, C if wide else 1, 0)

    for load in loads:
        load.wait()
    for i in range(C):
        qs[i] = rs_ref[1, :, i * r:(i + 1) * r].astype(BF16)
    q0[0, c] = qs[c]
    g0[0, c] = fill_ref[1, 0]

    def columns(i):
        return pl.ds(pl.multiple_of(i * r, r), r)

    def piece(i):
        return pl.ds(pl.multiple_of(i * b, b), b)

    st[c] = rs_ref[0, :, columns(c)]
    for side in range(2):
        @pl.when(sends(last, side))
        def _():
            g[last - 1, side, c] = fill_ref[0, side]

    pl.semaphore_wait(barrier, count)

    def rcopy(src, dst, ss, rr, pt, pc):
        return pltpu.make_async_remote_copy(
            src_ref=src, dst_ref=dst, send_sem=ss, recv_sem=rr, device_id=(pt, pc), device_id_type=MESH)

    def passed(j):
        return lax.rem(c - 2 * j + C, C)

    def own_fill(i):
        ss, rr = ab_s.at[0, i], ab_r.at[0, i]
        if i < H:
            return rcopy(fill_ref.at[1, 0], g0.at[0, c], ss, rr, p, peers[2 * i] if i else partner)
        slot = g0.at[0, passed(i - H + 1)]
        return rcopy(slot, slot, ss, rr, p, partner)

    def own_q(off):
        return rcopy(qs.at[peers[off]], q0.at[0, c], ab_s.at[1, off - 1], ab_r.at[1, off - 1], p, peers[off])

    def next_fill(i):
        ss, rr = cd_s.at[0, i], cd_r.at[0, i]
        if i < H:
            return rcopy(fill_ref.at[1, 1], g0.at[1, c], ss, rr, p + 1, peers[2 * i] if i else c)
        slot = g0.at[1, passed(i - H)]
        return rcopy(slot, slot, ss, rr, p, partner)

    def next_q(off):
        pc = c if off == 0 else peers[off]
        return rcopy(qs.at[pc], q0.at[1, c], cd_s.at[1, off], cd_r.at[1, off], p + 1, pc)

    def state_copy(off):
        return rcopy(rs_ref.at[0, :, columns(peers[off])], st.at[c], st_s.at[off - 1], st_r.at[off - 1], p, peers[off])

    def fill_piece(k, side):
        return rcopy(fill_ref.at[0, side], g.at[k - 1, side, c], fp_s.at[side], fp_r.at[k - 1, side], to(k, side), c)

    def forward(k, side, i):
        slot = g.at[k - 1, side, c if i < H else passed(i - H + 1)]
        pc = partner if i == 0 or i >= H else peers[2 * i]
        return rcopy(slot, slot, fw_s.at[k - 1, side, i], fw_r.at[k - 1, side, i], p, pc)

    def relay(copy):
        for i in range(1, H):
            copy(i).wait_recv()
            copy(H + i - 1).start()

    later = lax.rem(p, 2 ** last) > 0
    has_right, has_left = p + 1 < T, p >= 1

    def start_next_fill():
        @pl.when(has_right)
        def _():
            for i in reversed(range(H)):
                next_fill(i).start()

    def start_next_q():
        @pl.when(has_right)
        def _():
            for off in offs + [0]:
                next_q(off).start()

    def start_own_fill():
        for i in reversed(range(H)):
            own_fill(i).start()

    def start_own_q():
        for off in offs:
            own_q(off).start()

    def start_state():
        @pl.when(later)
        def _():
            for off in offs:
                state_copy(off).start()

    def start_pieces(k):
        for side in (1, 0):
            @pl.when(sends(k, side))
            def _():
                fill_piece(k, side).start()

    @pl.when(is_source(1))
    def _():
        start_own_fill()
        start_own_q()
        start_state()
        start_pieces(1)
        start_next_fill()
        start_next_q()

    @pl.when(is_kept(1))
    def _():
        start_next_fill()
        start_own_fill()
        start_next_q()
        start_own_q()
        for k in range(2, last):
            start_pieces(k)
        start_state()

    for k in range(1, last):
        for side in range(2):
            @pl.when(receives(k, side))
            def _():
                fill_piece(k, side).wait_recv()
                for i in reversed(range(H)):
                    forward(k, side, i).start()

    for side in range(2):
        @pl.when(sends(last, side))
        def _():
            for i in reversed(range(H)):
                forward(last, side, i).start()

    def whole(ref):
        return jnp.concatenate([ref[i] for i in range(C)], axis=0)

    def dot(f, q):
        return jnp.dot(f, q, preferred_element_type=F32)

    relay(own_fill)

    @pl.when(has_left)
    def _():
        for i in range(H):
            next_fill(i).wait_recv()
            next_fill(H + i).start()

    for i in rest:
        own_fill(i).wait_recv()
    for off in offs:
        own_q(off).wait_recv()
    acc[...] = dot(whole(g0.at[0]).T, whole(q0.at[0]))

    @pl.when(has_left)
    def _():
        for i in range(H, C):
            next_fill(i).wait_recv()
        for off in [0] + offs:
            next_q(off).wait_recv()
        acc[...] += dot(whole(g0.at[1]).T, whole(q0.at[1]))

    for k in range(1, LEVELS):
        for side in range(2):
            @pl.when(receives(k, side) if k < last else sends(k, side))
            def _():
                relay(functools.partial(forward, k, side))

    def out_copy(off):
        return rcopy(acc.at[piece(peers[off])], ao.at[c], ao_s.at[off - 1], ao_r.at[off - 1], p, peers[off])

    def start_out():
        for off in offs:
            out_copy(off).start()
        ao[c] = acc[piece(c)]

    m = H * b

    def chain_copy(k, side, h):
        rows = pl.ds(h * m, m)
        return rcopy(qb.at[rows], qv.at[k - 1, side, rows], ch_s.at[side, h], ch_r.at[k - 1, side, h], to(k, side), c)

    def final_copy(side, i):
        return rcopy(cs.at[side, piece(i)], fin.at[side, c], fi_s.at[side, i], fi_r.at[side, c], to(last, side), i)

    def final_recv(side, i):
        return rcopy(cs.at[side, piece(0)], fin.at[side, i], fi_s.at[side, i], fi_r.at[side, i], p, i)

    @pl.when(later)
    def _():
        for off in offs:
            state_copy(off).wait_recv()

    for k in range(1, LEVELS):
        if k == last - 1:
            for side in range(2):
                @pl.when(sends(last, side))
                def _():
                    for i in rest:
                        forward(last, side, i).wait_recv()
                    tl[side] = whole(g.at[last - 1, side]).T

        if k < last:
            for side in range(2):
                @pl.when(receives(k, side))
                def _():
                    for i in rest:
                        forward(k, side, i).wait_recv()
                    tf[side] = whole(g.at[k - 1, side]).T

        @pl.when(is_source(k))
        def _():
            if k < last:
                for h in range(2):
                    for i in range(h * H, (h + 1) * H):
                        qb[i * b:(i + 1) * b] = (st[i] - acc[i * b:(i + 1) * b]).astype(BF16)
                    for side in (1, 0):
                        @pl.when(target(k, side))
                        def _():
                            chain_copy(k, side, h).start()
            else:
                qk = (whole(st) - acc[...]).astype(BF16)
                for side in (1, 0):
                    @pl.when(target(k, side))
                    def _():
                        for h in range(2):
                            cs[side, h * m:(h + 1) * m] = dot(tl[side, h * m:(h + 1) * m], qk)
                            for i in range(h * H, (h + 1) * H):
                                final_copy(side, i).start()

            start_out()

        if k < last:
            for h in range(2):
                for side in range(2):
                    @pl.when(receives(k, side))
                    def _():
                        chain_copy(k, side, h).wait_recv()
                        acc[...] += dot(tf[side, :, h * m:(h + 1) * m], qv[k - 1, side, h * m:(h + 1) * m])
        else:
            @pl.when(is_kept(k))
            def _():
                start_out()

    for off in offs:
        out_copy(off).wait_recv()
    for i in range(C):
        out_ref[:, i * r:(i + 1) * r] = ao[i]
    for side in range(2):
        @pl.when(receives(last, side))
        def _():
            for i in range(C):
                final_recv(side, i).wait_recv()
                out_ref[:, i * r:(i + 1) * r] += fin[side, i]

    for i in range(C - 1):
        own_fill(i).wait_send()
    for off in offs:
        own_q(off).wait_send()
        out_copy(off).wait_send()

    @pl.when(has_right)
    def _():
        for i in range(H):
            next_fill(i).wait_send()
        for off in [0] + offs:
            next_q(off).wait_send()

    @pl.when(has_left)
    def _():
        for i in range(H, C):
            next_fill(i).wait_send()

    @pl.when(later)
    def _():
        for off in offs:
            state_copy(off).wait_send()

    for k in range(1, LEVELS):
        for side in range(2):
            @pl.when(sends(k, side))
            def _():
                if k == last:
                    for i in range(C):
                        final_copy(side, i).wait_send()
                    for i in range(C - 1):
                        forward(k, side, i).wait_send()
                else:
                    fill_piece(k, side).wait_send()
                    chain_copy(k, side, 0).wait_send()
                    chain_copy(k, side, 1).wait_send()

            if k < last:
                @pl.when(receives(k, side))
                def _():
                    for i in range(C - 1):
                        forward(k, side, i).wait_send()


def shards(T, C, right_sides, fill_blocks):
    _, b, R = right_sides.shape
    B = fill_blocks.shape[2]
    r = R // C
    n = fill_blocks.shape[3]
    dma = pltpu.SemaphoreType.DMA
    vm = pl.BlockSpec(memory_space=pltpu.VMEM)
    update = pl.pallas_call(
        functools.partial(kernel, T, C),
        out_shape=jax.ShapeDtypeStruct((b, R), F32),
        in_specs=[pl.BlockSpec(memory_space=pl.ANY)] * 2,
        out_specs=vm,
        scratch_shapes=[
            pltpu.VMEM(right_sides.shape, F32),
            pltpu.VMEM((2, 2, n, B), BF16),
            dma((3,)),
            pltpu.VMEM((2, C, n, B), BF16),
            pltpu.VMEM((C, b, r), BF16),
            pltpu.VMEM((2, C, b, r), BF16),
            pltpu.VMEM((C, b, r), F32),
            pltpu.VMEM((B, r), F32),
            pltpu.VMEM((LEVELS - 1, 2, C, n, B), BF16),
            pltpu.VMEM((2, B, B), BF16),
            pltpu.VMEM((2, B, B), BF16),
            pltpu.VMEM((B, r), BF16),
            pltpu.VMEM((LEVELS - 2, 2, B, r), BF16),
            pltpu.VMEM((2, B, r), F32),
            pltpu.VMEM((2, C, b, r), F32),
            pltpu.VMEM((C, b, r), F32),
            dma((2, C - 1)), dma((2, C - 1)),
            dma((2, C)), dma((2, C)),
            dma((C - 1,)), dma((C - 1,)),
            dma((2,)), dma((LEVELS - 2, 2)),
            dma((LEVELS - 1, 2, C - 1)), dma((LEVELS - 1, 2, C - 1)),
            dma((2, 2)), dma((LEVELS - 2, 2, 2)),
            dma((2, C)), dma((2, C)),
            dma((C - 1,)), dma((C - 1,)),
        ],
        compiler_params=pltpu.CompilerParams(collective_id=0, has_side_effects=True),
    )(right_sides, jnp.swapaxes(fill_blocks, 2, 3))
    return right_sides - jnp.pad(update[None], ((0, 1), (0, 0), (0, 0)))


def solution(mesh):
    placed = (P("turn", "col", None), P("turn", None, None, "col"))
    return jax.shard_map(
        functools.partial(shards, mesh.shape["turn"], mesh.shape["col"]),
        mesh=mesh, in_specs=placed, out_specs=P("turn", "col", None), check_vma=False
    )
```

```python
import functools

import jax
import jax.numpy as jnp
from jax import lax
from jax.experimental import pallas as pl
from jax.experimental.pallas import tpu as pltpu
from jax.sharding import PartitionSpec as P

LEVELS = 4
MESH = pl.DeviceIdType.MESH
F32 = jnp.float32
BF16 = jnp.bfloat16


def kernel(T, C, rs_hbm, fill_hbm, out_ref, rs_ref, fill_ref, in_s, g0, qs, q0, st, acc, g, tf, tl, qb, qv, cs, fin, ao,
           ab_s, ab_r, cd_s, cd_r, st_s, st_r, fp_s, fp_r, fw_s, fw_r, ch_s, ch_r, fi_s, fi_r, ao_s, ao_r):
    b, r = st.shape[1], st.shape[2]
    p, c = lax.axis_index("turn"), lax.axis_index("col")
    last = LEVELS - 1
    offs = list(range(1, C))
    peers = [None] + [lax.rem(c + off, C) for off in offs]
    H = C // 2
    partner = c + 1 - 2 * lax.rem(c, 2)
    rest = [0] + list(range(H, C - 1))

    def is_source(k):
        d = 2 ** (k - 1)
        return lax.rem(p, 2 * d) == d

    def is_kept(k):
        return lax.rem(p, 2 ** k) == 0

    def in_level(k):
        return lax.rem(p, 2 ** (k - 1)) == 0

    def to(k, side):
        d = 2 ** (k - 1)
        return p - d if side == 0 else p + d

    def target(k, side):
        d = 2 ** (k - 1)
        return p >= d if side == 0 else p + d < T

    def sends(k, side):
        return jnp.logical_and(is_source(k), target(k, side))

    def receives(k, side):
        return jnp.logical_and(is_kept(k), target(k, 1 - side))

    loads = [pltpu.make_async_copy(rs_hbm.at[1], rs_ref.at[1], in_s.at[0]),
             pltpu.make_async_copy(fill_hbm, fill_ref, in_s.at[1]),
             pltpu.make_async_copy(rs_hbm.at[0], rs_ref.at[0], in_s.at[2])]
    for load in loads:
        load.start()

    barrier = pltpu.get_barrier_semaphore()

    def greet(pt, pc):
        pl.semaphore_signal(barrier, inc=1, device_id=(pt, pc), device_id_type=MESH)

    for off in offs:
        greet(p, peers[off])
    count = jnp.int32(C - 1)
    for k in range(1, LEVELS):
        wide = k == 1 or k == last
        for side in range(2):
            cond = jnp.logical_and(in_level(k), target(k, side))

            @pl.when(cond)
            def _():
                greet(to(k, side), c)
                if wide:
                    for off in offs:
                        greet(to(k, side), peers[off])

            count = count + jnp.where(cond, C if wide else 1, 0)

    for load in loads:
        load.wait()
    for i in range(C):
        qs[i] = rs_ref[1, :, i * r:(i + 1) * r].astype(BF16)
    q0[0, c] = qs[c]
    g0[0, c] = fill_ref[1, 0]

    def columns(i):
        return pl.ds(pl.multiple_of(i * r, r), r)

    def piece(i):
        return pl.ds(pl.multiple_of(i * b, b), b)

    st[c] = rs_ref[0, :, columns(c)]
    for side in range(2):
        @pl.when(sends(last, side))
        def _():
            g[last - 1, side, c] = fill_ref[0, side]

    pl.semaphore_wait(barrier, count)

    def rcopy(src, dst, ss, rr, pt, pc):
        return pltpu.make_async_remote_copy(
            src_ref=src, dst_ref=dst, send_sem=ss, recv_sem=rr, device_id=(pt, pc), device_id_type=MESH)

    def passed(j):
        return lax.rem(c - 2 * j + C, C)

    def own_fill(i):
        ss, rr = ab_s.at[0, i], ab_r.at[0, i]
        if i < H:
            return rcopy(fill_ref.at[1, 0], g0.at[0, c], ss, rr, p, peers[2 * i] if i else partner)
        slot = g0.at[0, passed(i - H + 1)]
        return rcopy(slot, slot, ss, rr, p, partner)

    def own_q(off):
        return rcopy(qs.at[peers[off]], q0.at[0, c], ab_s.at[1, off - 1], ab_r.at[1, off - 1], p, peers[off])

    def next_fill(i):
        ss, rr = cd_s.at[0, i], cd_r.at[0, i]
        if i < H:
            return rcopy(fill_ref.at[1, 1], g0.at[1, c], ss, rr, p + 1, peers[2 * i] if i else c)
        slot = g0.at[1, passed(i - H)]
        return rcopy(slot, slot, ss, rr, p, partner)

    def next_q(off):
        pc = c if off == 0 else peers[off]
        return rcopy(qs.at[pc], q0.at[1, c], cd_s.at[1, off], cd_r.at[1, off], p + 1, pc)

    def state_copy(off):
        return rcopy(rs_ref.at[0, :, columns(peers[off])], st.at[c], st_s.at[off - 1], st_r.at[off - 1], p, peers[off])

    def fill_piece(k, side):
        return rcopy(fill_ref.at[0, side], g.at[k - 1, side, c], fp_s.at[side], fp_r.at[k - 1, side], to(k, side), c)

    def forward(k, side, i):
        slot = g.at[k - 1, side, c if i < H else passed(i - H + 1)]
        pc = partner if i == 0 or i >= H else peers[2 * i]
        return rcopy(slot, slot, fw_s.at[k - 1, side, i], fw_r.at[k - 1, side, i], p, pc)

    def relay(copy):
        for i in range(1, H):
            copy(i).wait_recv()
            copy(H + i - 1).start()

    later = lax.rem(p, 2 ** last) > 0
    has_right, has_left = p + 1 < T, p >= 1

    @pl.when(has_right)
    def _():
        for i in reversed(range(H)):
            next_fill(i).start()

    for i in reversed(range(H)):
        own_fill(i).start()

    @pl.when(has_right)
    def _():
        for off in offs + [0]:
            next_q(off).start()

    for off in offs:
        own_q(off).start()
    for k in range(1, last):
        for side in (1, 0):
            @pl.when(sends(k, side))
            def _():
                fill_piece(k, side).start()

    @pl.when(later)
    def _():
        for off in offs:
            state_copy(off).start()

    for k in range(1, last):
        for side in range(2):
            @pl.when(receives(k, side))
            def _():
                fill_piece(k, side).wait_recv()
                for i in reversed(range(H)):
                    forward(k, side, i).start()

    for side in range(2):
        @pl.when(sends(last, side))
        def _():
            for i in reversed(range(H)):
                forward(last, side, i).start()

    def whole(ref):
        return jnp.concatenate([ref[i] for i in range(C)], axis=0)

    def dot(f, q):
        return jnp.dot(f, q, preferred_element_type=F32)

    relay(own_fill)

    @pl.when(has_left)
    def _():
        for i in range(H):
            next_fill(i).wait_recv()
            next_fill(H + i).start()

    for i in rest:
        own_fill(i).wait_recv()
    for off in offs:
        own_q(off).wait_recv()
    acc[...] = dot(whole(g0.at[0]).T, whole(q0.at[0]))

    @pl.when(has_left)
    def _():
        for i in range(H, C):
            next_fill(i).wait_recv()
        for off in [0] + offs:
            next_q(off).wait_recv()
        acc[...] += dot(whole(g0.at[1]).T, whole(q0.at[1]))

    for k in range(1, LEVELS):
        for side in range(2):
            @pl.when(receives(k, side) if k < last else sends(k, side))
            def _():
                relay(functools.partial(forward, k, side))

    def out_copy(off):
        return rcopy(acc.at[piece(peers[off])], ao.at[c], ao_s.at[off - 1], ao_r.at[off - 1], p, peers[off])

    def start_out():
        for off in offs:
            out_copy(off).start()
        ao[c] = acc[piece(c)]

    def chain_copy(k, side):
        return rcopy(qb, qv.at[k - 1, side], ch_s.at[side], ch_r.at[k - 1, side], to(k, side), c)

    def final_copy(side, i):
        return rcopy(cs.at[side, piece(i)], fin.at[side, c], fi_s.at[side, i], fi_r.at[side, c], to(last, side), i)

    def final_recv(side, i):
        return rcopy(cs.at[side, piece(0)], fin.at[side, i], fi_s.at[side, i], fi_r.at[side, i], p, i)

    @pl.when(later)
    def _():
        for off in offs:
            state_copy(off).wait_recv()

    for k in range(1, LEVELS):
        if k == last - 1:
            for side in range(2):
                @pl.when(sends(last, side))
                def _():
                    for i in rest:
                        forward(last, side, i).wait_recv()
                    tl[side] = whole(g.at[last - 1, side]).T

        if k < last:
            for side in range(2):
                @pl.when(receives(k, side))
                def _():
                    for i in rest:
                        forward(k, side, i).wait_recv()
                    tf[side] = whole(g.at[k - 1, side]).T

        @pl.when(is_source(k))
        def _():
            qk = (whole(st) - acc[...]).astype(BF16)
            if k < last:
                qb[...] = qk
            for side in (1, 0):
                @pl.when(target(k, side))
                def _():
                    if k == last:
                        cs[side] = dot(tl[side], qk)
                        for j in reversed(range(H)):
                            to_col = peers[2 * j] if j else c
                            final_copy(side, to_col).start()
                            final_copy(side, to_col + 1 - 2 * lax.rem(to_col, 2)).start()
                    else:
                        chain_copy(k, side).start()

            start_out()

        if k < last:
            for side in range(2):
                @pl.when(receives(k, side))
                def _():
                    chain_copy(k, side).wait_recv()
                    acc[...] += dot(tf[side], qv[k - 1, side])
        else:
            @pl.when(is_kept(k))
            def _():
                start_out()

    for off in offs:
        out_copy(off).wait_recv()
    for i in range(C):
        out_ref[:, i * r:(i + 1) * r] = ao[i]
    for side in range(2):
        @pl.when(receives(last, side))
        def _():
            for i in range(C):
                final_recv(side, i).wait_recv()
                out_ref[:, i * r:(i + 1) * r] += fin[side, i]

    for i in range(C - 1):
        own_fill(i).wait_send()
    for off in offs:
        own_q(off).wait_send()
        out_copy(off).wait_send()

    @pl.when(has_right)
    def _():
        for i in range(H):
            next_fill(i).wait_send()
        for off in [0] + offs:
            next_q(off).wait_send()

    @pl.when(has_left)
    def _():
        for i in range(H, C):
            next_fill(i).wait_send()

    @pl.when(later)
    def _():
        for off in offs:
            state_copy(off).wait_send()

    for k in range(1, LEVELS):
        for side in range(2):
            @pl.when(sends(k, side))
            def _():
                if k == last:
                    for i in range(C):
                        final_copy(side, i).wait_send()
                    for i in range(C - 1):
                        forward(k, side, i).wait_send()
                else:
                    fill_piece(k, side).wait_send()
                    chain_copy(k, side).wait_send()

            if k < last:
                @pl.when(receives(k, side))
                def _():
                    for i in range(C - 1):
                        forward(k, side, i).wait_send()


def shards(T, C, right_sides, fill_blocks):
    _, b, R = right_sides.shape
    B = fill_blocks.shape[2]
    r = R // C
    n = fill_blocks.shape[3]
    dma = pltpu.SemaphoreType.DMA
    vm = pl.BlockSpec(memory_space=pltpu.VMEM)
    update = pl.pallas_call(
        functools.partial(kernel, T, C),
        out_shape=jax.ShapeDtypeStruct((b, R), F32),
        in_specs=[pl.BlockSpec(memory_space=pl.ANY)] * 2,
        out_specs=vm,
        scratch_shapes=[
            pltpu.VMEM(right_sides.shape, F32),
            pltpu.VMEM((2, 2, n, B), BF16),
            dma((3,)),
            pltpu.VMEM((2, C, n, B), BF16),
            pltpu.VMEM((C, b, r), BF16),
            pltpu.VMEM((2, C, b, r), BF16),
            pltpu.VMEM((C, b, r), F32),
            pltpu.VMEM((B, r), F32),
            pltpu.VMEM((LEVELS - 1, 2, C, n, B), BF16),
            pltpu.VMEM((2, B, B), BF16),
            pltpu.VMEM((2, B, B), BF16),
            pltpu.VMEM((B, r), BF16),
            pltpu.VMEM((LEVELS - 2, 2, B, r), BF16),
            pltpu.VMEM((2, B, r), F32),
            pltpu.VMEM((2, C, b, r), F32),
            pltpu.VMEM((C, b, r), F32),
            dma((2, C - 1)), dma((2, C - 1)),
            dma((2, C)), dma((2, C)),
            dma((C - 1,)), dma((C - 1,)),
            dma((2,)), dma((LEVELS - 2, 2)),
            dma((LEVELS - 1, 2, C - 1)), dma((LEVELS - 1, 2, C - 1)),
            dma((2,)), dma((LEVELS - 2, 2)),
            dma((2, C)), dma((2, C)),
            dma((C - 1,)), dma((C - 1,)),
        ],
        compiler_params=pltpu.CompilerParams(collective_id=0, has_side_effects=True),
    )(right_sides, jnp.swapaxes(fill_blocks, 2, 3))
    return right_sides - jnp.pad(update[None], ((0, 1), (0, 0), (0, 0)))


def solution(mesh):
    placed = (P("turn", "col", None), P("turn", None, None, "col"))
    return jax.shard_map(
        functools.partial(shards, mesh.shape["turn"], mesh.shape["col"]),
        mesh=mesh, in_specs=placed, out_specs=P("turn", "col", None), check_vma=False
    )
```
